512 devices in a mesh: gx: 32 (over y, x), gy: 16 (over z, core).
Axes of the slice: x: 4, y: 8, z: 8, core: 2. Of those that a mesh axis runs over, the one named last changes fastest.
Arguments:
- solution: float32 [32, 16, 8, 8, 8, 128], P('gx', 'gy'), as said below
- residual: float32 [32, 16, 8, 8, 8, 128], P('gx', 'gy'), as said below
- grain_counts: int32 [32, 16, 128], P('gx', 'gy'), may hold values from 0 to 16
Outputs:
- solution_out: float32 [32, 16, 8, 8, 8, 128], P('gx', 'gy')
- residual_out: float32 [32, 16, 8, 8, 8, 128], P('gx', 'gy')
- direction_out: float32 [32, 16, 8, 8, 8, 128], P('gx', 'gy')
- step_sizes: float32 [2], replicated
The draws below stay inside these ranges and needn't reach their ends.
Inputs may be any that keep to these rules, and one draw needn't show every extreme that they name: `solution`: every node shared by neighbouring elements holds the same value in all of its copies. `residual`: every node shared by neighbouring elements holds the same value in all of its copies.
All inputs are finite; a program needn't handle non-finite values.
Results may differ from the reference program's by a relative error of at most 0.003.
Values sent between devices are 32-bit elements; how exact they have to be, the bound alone decides.
A program may use at most 64 MiB of HBM per device.

```python
import math
import jax
import jax.numpy as jnp
import numpy as np
from jax import lax

NODES = 8
EZ = 128
MOST_GRAINS = 16
ITERS = 2
NXE = 32
NYE = 16


def continuous_field(key):
    span = NODES - 1
    grid_shape = (span * NXE + 1, span * NYE + 1, span * EZ + 1)
    grid = jax.random.normal(key, grid_shape, jnp.float32)
    along_first = jnp.stack([grid[offset:offset + span * NXE:span] for offset in range(NODES)], axis=1)
    along_second = jnp.stack([along_first[:, :, offset:offset + span * NYE:span] for offset in range(NODES)], axis=3)
    along_third = jnp.stack([along_second[..., offset:offset + span * EZ:span] for offset in range(NODES)], axis=5)
    return jnp.transpose(along_third, (0, 2, 1, 3, 5, 4))


def draw_solution(key, part):
    return continuous_field(jax.random.fold_in(key, 11))


def draw_residual(key, part):
    return continuous_field(jax.random.fold_in(key, 23))


def touch_ends(values, key, smallest, high):
    index_at = [jax.random.randint(jax.random.fold_in(key, axis), (), 0, length) for axis, length in enumerate(values.shape)]
    widest = values.shape.index(max(values.shape))
    next_to = index_at[:widest] + [(index_at[widest] + 1) % values.shape[widest]] + index_at[widest + 1:]
    return values.at[tuple(index_at)].set(smallest).at[tuple(next_to)].set(high)


def setup_inputs(seed: int = 0) -> dict:
    seeds = jax.random.split(jax.random.key(seed), 4)
    return {
        "solution": draw_solution(jax.random.fold_in(seeds[3], 71), 0),
        "residual": draw_residual(jax.random.fold_in(seeds[3], 71), 0),
        "grain_counts": touch_ends(jax.random.randint(seeds[2], (NXE, NYE, EZ), 0, MOST_GRAINS + 1), jax.random.fold_in(seeds[2], 1), 0, MOST_GRAINS).astype(jnp.int32),
    }


shift_mass = 0.1
mean_porosity = 0.7
exact_mode = lax.Precision.HIGHEST

def legendre_columns(node_set, degree):
    table = [node_set * 0.0 + 1.0, node_set]
    for order in range(2, degree + 1):
        table.append(((2 * order - 1) * node_set * table[order - 1] - (order - 1) * table[order - 2]) / order)
    return table

def gll_tables():
    degree = NODES - 1
    node_set = np.cos(math.pi * np.arange(degree + 1) / degree)
    for sweep in range(100):
        table = legendre_columns(node_set, degree)
        node_set = node_set - (node_set * table[degree] - table[degree - 1]) / ((degree + 1) * table[degree])
    node_set = node_set[::-1].copy()
    values = legendre_columns(node_set, degree)[degree]
    weights = 2.0 / (degree * (degree + 1) * values ** 2)
    derivative = np.zeros((NODES, NODES))
    for row_index in range(NODES):
        for column_index in range(NODES):
            if row_index != column_index:
                derivative[row_index, column_index] = values[row_index] / (values[column_index] * (node_set[row_index] - node_set[column_index]))
    derivative[0, 0] = -degree * (degree + 1) / 4.0
    derivative[NODES - 1, NODES - 1] = degree * (degree + 1) / 4.0
    return (weights, derivative)

def jacobi_eigen(matrix):
    size_now = matrix.shape[0]
    current = matrix.copy()
    vectors = np.eye(size_now)
    for sweep in range(12):
        for first in range(size_now - 1):
            for second in range(first + 1, size_now):
                off_value = current[first, second]
                safe_value = np.where(off_value == 0.0, 1e-300, off_value)
                theta = (current[second, second] - current[first, first]) / (2.0 * safe_value)
                sign_value = np.where(theta >= 0.0, 1.0, -1.0)
                tangent = sign_value / (np.abs(theta) + np.sqrt(theta * theta + 1.0))
                cosine = 1.0 / np.sqrt(tangent * tangent + 1.0)
                sine = tangent * cosine
                rotation = np.eye(size_now)
                rotation[first, first] = cosine
                rotation[second, second] = cosine
                rotation[first, second] = sine
                rotation[second, first] = -sine
                current = rotation.T @ current @ rotation
                vectors = vectors @ rotation
    eigen_values = np.array([current[index, index] for index in range(size_now)])
    return (eigen_values, vectors)

def schwarz_tables():
    weights, derivative = gll_tables()
    stiffness = derivative.T @ (weights[:, None] * derivative)
    total_nodes = 3 * (NODES - 1) + 1
    three_stiffness = np.zeros((total_nodes, total_nodes))
    three_mass = np.zeros(total_nodes)
    for element in range(3):
        start_node = element * (NODES - 1)
        three_stiffness[start_node:start_node + NODES, start_node:start_node + NODES] += stiffness
        three_mass[start_node:start_node + NODES] += weights
    chosen = np.array([NODES - 2] + list(range(NODES - 1, 2 * NODES - 1)) + [2 * NODES - 1])
    local_stiffness = three_stiffness[chosen][:, chosen]
    local_mass = three_mass[chosen]
    scaling = 1.0 / np.sqrt(local_mass)
    symmetric = scaling[:, None] * local_stiffness * scaling[None, :]
    symmetric = 0.5 * (symmetric + symmetric.T)
    eigen_values, eigen_vectors = jacobi_eigen(symmetric)
    return (scaling[:, None] * eigen_vectors, eigen_values)

def cosine_basis(column_count):
    position = jnp.arange(column_count, dtype=jnp.float32)
    phase_table = math.pi * (position[:, None] + 0.5) * position[None, :] / column_count
    norm_factor = jnp.where(position == 0, math.sqrt(1.0 / column_count), math.sqrt(2.0 / column_count))
    eigen_basis = jnp.cos(phase_table) * norm_factor[None, :]
    eigen_values = 2.0 - 2.0 * jnp.cos(math.pi * position / column_count)
    return (eigen_basis, eigen_values)

def coarse_solve(coarse_source, column_length):
    basis_first, eigen_first = cosine_basis(coarse_source.shape[0])
    basis_second, eigen_second = cosine_basis(coarse_source.shape[1])
    spectrum = jnp.einsum('pa,pq,qb->ab', basis_first, coarse_source, basis_second, precision=exact_mode)
    divisor = 2.0 * mean_porosity * column_length * (eigen_first[:, None] + eigen_second[None, :]) + 8.0 * shift_mass * column_length
    return jnp.einsum('pa,ab,qb->pq', basis_first, spectrum / divisor, basis_second, precision=exact_mode)

def share_weights(column_count, points):
    column = jnp.arange(column_count)
    identity = (column[:, None] == column[None, :]).astype(jnp.float32)
    left_side = (column[None, :] == column[:, None] - 1).astype(jnp.float32)
    right_side = (column[None, :] == column[:, None] + 1).astype(jnp.float32)
    has_left = (column > 0).astype(jnp.float32)
    has_right = (column < column_count - 1).astype(jnp.float32)
    lowest = identity * (1.0 - 0.5 * has_left[:, None]) + 0.5 * left_side
    highest = identity * (1.0 - 0.5 * has_right[:, None]) + 0.5 * right_side
    table = jnp.broadcast_to(identity[:, None, :], (column_count, points, column_count))
    return table.at[:, 0, :].set(lowest).at[:, points - 1, :].set(highest)

def multiplicity_inverse(column_count, points):
    column = jnp.arange(column_count)[:, None]
    node_index = jnp.arange(points)[None, :]
    shared = (node_index == 0) & (column > 0) | (node_index == points - 1) & (column < column_count - 1)
    return 1.0 / (1.0 + shared.astype(jnp.float32))

def shift_elements(layers, element_axis, toward):
    extent = layers.shape[element_axis]
    widths = [(0, 0)] * layers.ndim
    if toward > 0:
        retained = lax.slice_in_dim(layers, 0, extent - 1, axis=element_axis)
        widths[element_axis] = (1, 0)
    else:
        retained = lax.slice_in_dim(layers, 1, extent, axis=element_axis)
        widths[element_axis] = (0, 1)
    return jnp.pad(retained, widths)

def extend(nodal_field, node_axis, element_axis):
    points = nodal_field.shape[node_axis]
    lower_layer = shift_elements(lax.slice_in_dim(nodal_field, points - 2, points - 1, axis=node_axis), element_axis, 1)
    upper_layer = shift_elements(lax.slice_in_dim(nodal_field, 1, 2, axis=node_axis), element_axis, -1)
    return jnp.concatenate([lower_layer, nodal_field, upper_layer], axis=node_axis)

def spread(extended, node_axis, element_axis):
    points = extended.shape[node_axis] - 2
    own_part = lax.slice_in_dim(extended, 1, points + 1, axis=node_axis)
    lower_layer = shift_elements(lax.slice_in_dim(extended, points, points + 2, axis=node_axis), element_axis, 1)
    upper_layer = shift_elements(lax.slice_in_dim(extended, 0, 2, axis=node_axis), element_axis, -1)
    lower_widths = [(0, 0)] * extended.ndim
    lower_widths[node_axis] = (0, points - 2)
    upper_widths = [(0, 0)] * extended.ndim
    upper_widths[node_axis] = (points - 2, 0)
    return own_part + jnp.pad(lower_layer, lower_widths) + jnp.pad(upper_layer, upper_widths)

def schwarz_solve(extended, eigen_basis, eigen_values):
    first_pass = jnp.einsum('ia,...ijke->...ajke', eigen_basis, extended, precision=exact_mode)
    second_pass = jnp.einsum('jb,...ajke->...abke', eigen_basis, first_pass, precision=exact_mode)
    third_pass = jnp.einsum('kc,...abke->...abce', eigen_basis, second_pass, precision=exact_mode)
    divisor = mean_porosity * (eigen_values[:, None, None] + eigen_values[None, :, None] + eigen_values[None, None, :]) + shift_mass
    scaled = third_pass / divisor[..., None]
    back_first = jnp.einsum('ia,...abce->...ibce', eigen_basis, scaled, precision=exact_mode)
    back_second = jnp.einsum('jb,...ibce->...ijce', eigen_basis, back_first, precision=exact_mode)
    return jnp.einsum('kc,...ijce->...ijke', eigen_basis, back_second, precision=exact_mode)

def apply_local(nodal_field, coupling, derivative, weights_cube):
    grad_first = jnp.einsum('ai,...ijke->...ajke', derivative, nodal_field, precision=exact_mode)
    flux_first = jnp.einsum('ai,...ajke->...ijke', derivative, coupling * grad_first, precision=exact_mode)
    grad_second = jnp.einsum('bj,...ijke->...ibke', derivative, nodal_field, precision=exact_mode)
    flux_second = jnp.einsum('bj,...ibke->...ijke', derivative, coupling * grad_second, precision=exact_mode)
    grad_third = jnp.einsum('ck,...ijke->...ijce', derivative, nodal_field, precision=exact_mode)
    flux_third = jnp.einsum('ck,...ijce->...ijke', derivative, coupling * grad_third, precision=exact_mode)
    return flux_first + flux_second + flux_third + shift_mass * weights_cube[..., None] * nodal_field

def assemble_z(nodal_field):
    points = nodal_field.shape[-2]
    shared = nodal_field[..., points - 1, :-1] + nodal_field[..., 0, 1:]
    return nodal_field.at[..., points - 1, :-1].set(shared).at[..., 0, 1:].set(shared)

def assemble(nodal_field):
    points = nodal_field.shape[2]
    shared = nodal_field[:-1, :, points - 1] + nodal_field[1:, :, 0]
    nodal_field = nodal_field.at[:-1, :, points - 1].set(shared).at[1:, :, 0].set(shared)
    shared = nodal_field[:, :-1, :, points - 1] + nodal_field[:, 1:, :, 0]
    nodal_field = nodal_field.at[:, :-1, :, points - 1].set(shared).at[:, 1:, :, 0].set(shared)
    return assemble_z(nodal_field)

def reference(solution, residual, grain_counts):
    weights_np, derivative_np = gll_tables()
    weights = jnp.asarray(weights_np, dtype=jnp.float32)
    derivative = jnp.asarray(derivative_np, dtype=jnp.float32)
    weights_cube = weights[:, None, None] * weights[None, :, None] * weights[None, None, :]
    basis_np, eigen_np = schwarz_tables()
    eigen_basis = jnp.asarray(basis_np, dtype=jnp.float32)
    eigen_values = jnp.asarray(eigen_np, dtype=jnp.float32)
    porosity = 1.0 - 0.6 * grain_counts.astype(jnp.float32) / MOST_GRAINS
    coupling = weights_cube[None, None, :, :, :, None] * porosity[:, :, None, None, None, :]
    inverse_first = multiplicity_inverse(NXE, NODES)
    inverse_second = multiplicity_inverse(NYE, NODES)
    inverse_third = multiplicity_inverse(EZ, NODES).T
    inverse_all = inverse_first[:, None, :, None, None, None] * inverse_second[None, :, None, :, None, None] * inverse_third[None, None, None, None, :, :]
    share_first = share_weights(NXE, NODES)
    share_second = share_weights(NYE, NODES)

    def precondition(residual_now):
        extended = extend(extend(extend(residual_now, 2, 0), 3, 1), 4, 5)
        local_solution = schwarz_solve(extended, eigen_basis, eigen_values)
        schwarz_part = spread(spread(spread(local_solution, 2, 0), 3, 1), 4, 5)
        columns = lax.optimization_barrier(jnp.sum(inverse_all * residual_now, axis=(4, 5)))
        coarse_source = jnp.einsum('xyij,xia,yjb->ab', columns, share_first, share_second, precision=exact_mode)
        coarse_field = coarse_solve(coarse_source, EZ)
        lifted = jnp.einsum('xia,ab,yjb->xyij', share_first, coarse_field, share_second, precision=exact_mode)
        return schwarz_part + lifted[..., None, None]
    direction = residual
    previous_inner = jnp.float32(1.0)
    step_list = []
    for step_index in range(ITERS):
        preconditioned = precondition(residual)
        precond_inner = jnp.sum(inverse_all * residual * preconditioned)
        if step_index == 0:
            direction = preconditioned
        else:
            direction = preconditioned + precond_inner / previous_inner * direction
        image = assemble(apply_local(direction, coupling, derivative, weights_cube))
        step_size = precond_inner / jnp.sum(inverse_all * direction * image)
        solution = solution + step_size * direction
        residual = residual - step_size * image
        previous_inner = precond_inner
        step_list.append(step_size)
    return (solution, residual, direction, jnp.stack(step_list))
```

```python
import functools
import math

import jax
import jax.numpy as jnp
import ml_dtypes
import numpy as np
from jax import lax
from jax.experimental import pallas as pl
from jax.experimental.pallas import tpu as pltpu
from jax.sharding import PartitionSpec as P

N = 8
MOST_GRAINS = 16
shift_mass = 0.1
mean_porosity = 0.7
MESH = pl.DeviceIdType.MESH
F32 = jnp.float32
BF16 = jnp.bfloat16
MOVES = [(1, 0), (-1, 0), (0, 1), (0, -1), (1, 1), (1, -1), (-1, 1), (-1, -1)]
PLAIN = 48


def legendre_columns(node_set, degree):
    table = [node_set * 0.0 + 1.0, node_set]
    for order in range(2, degree + 1):
        table.append(((2 * order - 1) * node_set * table[order - 1] - (order - 1) * table[order - 2]) / order)
    return table


def gll_tables():
    degree = N - 1
    node_set = np.cos(math.pi * np.arange(degree + 1) / degree)
    for _ in range(100):
        table = legendre_columns(node_set, degree)
        node_set = node_set - (node_set * table[degree] - table[degree - 1]) / ((degree + 1) * table[degree])
    node_set = node_set[::-1].copy()
    values = legendre_columns(node_set, degree)[degree]
    weights = 2.0 / (degree * (degree + 1) * values**2)
    derivative = np.zeros((N, N))
    for a in range(N):
        for b in range(N):
            if a != b:
                derivative[a, b] = values[a] / (values[b] * (node_set[a] - node_set[b]))
    derivative[0, 0] = -degree * (degree + 1) / 4.0
    derivative[N - 1, N - 1] = degree * (degree + 1) / 4.0
    return weights, derivative


def schwarz_tables():
    weights, derivative = gll_tables()
    stiffness = derivative.T @ (weights[:, None] * derivative)
    total = 3 * (N - 1) + 1
    three_stiffness = np.zeros((total, total))
    three_mass = np.zeros(total)
    for element in range(3):
        at = element * (N - 1)
        three_stiffness[at : at + N, at : at + N] += stiffness
        three_mass[at : at + N] += weights
    chosen = np.array([N - 2] + list(range(N - 1, 2 * N - 1)) + [2 * N - 1])
    scaling = 1.0 / np.sqrt(three_mass[chosen])
    symmetric = scaling[:, None] * three_stiffness[chosen][:, chosen] * scaling[None, :]
    values, vectors = np.linalg.eigh(0.5 * (symmetric + symmetric.T))
    return scaling[:, None] * vectors, values


def hi_lo(matrix):
    high = matrix.astype(ml_dtypes.bfloat16)
    low = (matrix - high.astype(np.float64)).astype(ml_dtypes.bfloat16)
    return np.concatenate([high, low], axis=-2)


def schwarz_blocks():
    basis, values = schwarz_tables()
    m = N + 2
    divisor = mean_porosity * (values[:, None, None] + values[None, :, None] + values[None, None, :]) + shift_mass
    fold = np.zeros((2, m // 2, m))
    for i in range(m // 2):
        fold[0, i, i] = fold[0, i, m - 1 - i] = 1.0
        fold[1, i, i], fold[1, i, m - 1 - i] = 1.0, -1.0
    order = np.zeros((m // 2, m // 2, m), np.int64)
    for i in range(m // 2):
        for j in range(m // 2):
            at = i * (m // 2) + j
            order[i, j, 1 : m - 1] = at * N + np.arange(N)
            order[i, j, 0] = (m // 2) ** 2 * N + at
            order[i, j, m - 1] = (m // 2) ** 2 * (N + 1) + at
    order = order.reshape(-1)
    blocks = np.zeros((4, 256, 256))
    for p in range(2):
        for q in range(2):
            left = np.kron(np.kron(fold[p] @ basis, fold[q] @ basis), basis)
            block = (left / divisor.reshape(-1)) @ left.T / 16.0
            blocks[2 * p + q][np.ix_(order, order)] = block
    return hi_lo(blocks)


def stiffness_blocks():
    weights, derivative = gll_tables()
    one = derivative.T @ (weights[:, None] * derivative)
    mass = np.diag(weights)
    whole = (
        np.kron(np.kron(one, mass), mass) + np.kron(np.kron(mass, one), mass) + np.kron(np.kron(mass, mass), one)
    )
    half = N // 2 * N * N
    blocks = np.zeros((2, half, half))
    for p, sign in enumerate((1.0, -1.0)):
        fold = np.zeros((N // 2, N))
        for i in range(N // 2):
            fold[i, i], fold[i, N - 1 - i] = 1.0, sign
        fold = np.kron(fold, np.eye(N * N))
        blocks[p] = fold @ whole @ fold.T / 4.0
    return hi_lo(blocks)


def cosine_basis(count):
    position = np.arange(count, dtype=np.float64)
    phase = math.pi * (position[:, None] + 0.5) * position[None, :] / count
    norm = np.where(position == 0, math.sqrt(1.0 / count), math.sqrt(2.0 / count))
    return np.cos(phase) * norm[None, :], 2.0 - 2.0 * np.cos(math.pi * position / count)


def share_rows(count):
    table = np.zeros((count, 3, count))
    for at in range(count):
        table[at, :, at] = 1.0
        if at > 0:
            table[at, 0, at], table[at, 0, at - 1] = 0.5, 0.5
        if at < count - 1:
            table[at, 2, at], table[at, 2, at + 1] = 0.5, 0.5
    return table


def coarse_tables(nx, ny, length):
    first, eigen_first = cosine_basis(nx)
    second, eigen_second = cosine_basis(ny)
    divisor = (
        2.0 * mean_porosity * length * (eigen_first[:, None] + eigen_second[None, :]) + 8.0 * shift_mass * length
    )
    share_first, share_second = share_rows(nx), share_rows(ny)
    along_y = np.ones((ny, 128))
    along_x = np.ones((nx, nx, 128))
    green = np.einsum("ap,bp,pk->kab", first, first, 1.0 / divisor)
    back = np.zeros((ny, 16, 128))
    for t in range(3):
        lanes = slice(t * ny, (t + 1) * ny)
        along_y[:, lanes] = second
        along_x[:, :, lanes] = np.einsum("xc,kcb->xbk", share_first[:, t], green)
        for s in range(3):
            back[:, 3 * t + s, lanes] = share_second[:, s] @ second
    for row in range(3):
        back[:, 9 + row, PLAIN + 16 * row] = 1.0
    return along_y.astype(np.float32), along_x.astype(np.float32), back.astype(np.float32)


def mass_table():
    weights, _ = gll_tables()
    table = shift_mass * (weights[:, None] * weights[None, :]).reshape(N * N, 1)
    return np.broadcast_to(table, (N * N, 128)).astype(np.float32).copy()


def part(step, low, high, whole):
    return low if step < 0 else (high if step > 0 else whole)


def span(first, count, unit=1):
    return pl.ds(first * unit, count * unit)


def kernel(
    nx, ny, node_weights,
    sol_in, res_in, grains_in, schwarz_in, stiff_in, along_y_in, along_x_in, back_in, mass_in,
    sol_out, res_out, dir_out, steps_out,
    sol, ext0, ext1, grains, schwarz, stiff, along_y, along_x, back, mass,
    blk, oblk, ab, loc0, loc1, d, w, q1, qw, lift, msg, buf_y, buf_x, sv, sides, corners, sides1, corners1,
    z2, r1, im2,
    load_sem, send_sem, recv_sem, gy_send, gy_recv, gx_send, gx_recv,
):
    x, y = lax.axis_index("gx"), lax.axis_index("gy")

    def inside(dx, dy):
        checks = []
        if dx > 0:
            checks.append(x < nx - 1)
        if dx < 0:
            checks.append(x > 0)
        if dy > 0:
            checks.append(y < ny - 1)
        if dy < 0:
            checks.append(y > 0)
        return functools.reduce(jnp.logical_and, checks)

    loads = [
        pltpu.make_async_copy(src, dst, load_sem.at[i])
        for i, (src, dst) in enumerate(
            [
                (res_in.at[0, 0], ext0.at[pl.ds(1, N), pl.ds(N, N * N)]),
                (schwarz_in, schwarz),
                (along_y_in, along_y),
                (along_x_in.at[x], along_x),
                (back_in.at[y], back),
                (grains_in.at[0], grains),
                (stiff_in, stiff),
                (mass_in, mass),
                (sol_in.at[0, 0], sol),
            ]
        )
    ]
    for load in loads:
        load.start()

    for m, (dx, dy) in enumerate(MOVES):

        @pl.when(jnp.logical_not(inside(-dx, -dy)))
        def _():
            for phase in range(3):
                incoming(sides, corners, phase, m)[...] = jnp.zeros_like(incoming(sides, corners, phase, m))
            edge = incoming(sides1, corners1, None, m)
            edge[...] = jnp.zeros_like(edge)
            area = ext0.at[span(*part(dx, (N + 1, 1), (0, 1), (1, N))), span(*part(dy, (N + 1, 1), (0, 1), (1, N)), N)]
            area[...] = jnp.zeros_like(area)

    barrier = pltpu.get_barrier_semaphore()

    @pl.loop(1, ny)
    def _(k):
        pl.semaphore_signal(barrier, inc=1, device_id=(x, lax.rem(y + k, ny)), device_id_type=MESH)

    @pl.loop(1, nx)
    def _(k):
        pl.semaphore_signal(barrier, inc=1, device_id=(lax.rem(x + k, nx), y), device_id_type=MESH)

    expected = jnp.int32(nx - 1 + ny - 1)
    for dx, dy in MOVES:
        if dx and dy:
            there = inside(dx, dy)
            expected = expected + there.astype(jnp.int32)

            @pl.when(there)
            def _():
                pl.semaphore_signal(barrier, inc=1, device_id=(x + dx, y + dy), device_id_type=MESH)

    pl.semaphore_wait(barrier, expected)

    def copies(phase, source, target):
        return [
            pltpu.make_async_remote_copy(
                src_ref=source(dx, dy),
                dst_ref=target(m),
                send_sem=send_sem.at[phase, m],
                recv_sem=recv_sem.at[phase, m],
                device_id=(x + dx, y + dy),
                device_id_type=MESH,
            )
            for m, (dx, dy) in enumerate(MOVES)
        ]

    def start(group):
        for m, (dx, dy) in enumerate(MOVES):
            pl.when(inside(dx, dy))(group[m].start)

    def arrive(group):
        for m, (dx, dy) in enumerate(MOVES):
            pl.when(inside(-dx, -dy))(group[m].wait_recv)

    def sent(group):
        for m, (dx, dy) in enumerate(MOVES):
            pl.when(inside(dx, dy))(group[m].wait_send)

    def ext_target(m):
        dx, dy = MOVES[m]
        return ext0.at[span(*part(dx, (N + 1, 1), (0, 1), (1, N))), span(*part(dy, (N + 1, 1), (0, 1), (1, N)), N)]

    halo0 = copies(
        0,
        lambda dx, dy: res_in.at[
            0, 0, span(*part(dx, (1, 1), (N - 2, 1), (0, N))), span(*part(dy, (1, 1), (N - 2, 1), (0, N)), N)
        ],
        ext_target,
    )
    start(halo0)

    lane = lax.broadcasted_iota(jnp.int32, (1, 128), 1)
    last = 127
    row = lax.broadcasted_iota(jnp.int32, (N * N, 128), 0)
    wide = lax.broadcasted_iota(jnp.int32, (N * N, 128), 1)
    inner = lax.rem(row, N)
    shared_z = ((inner == 0) & (wide > 0)) | ((inner == N - 1) & (wide < last))
    weight_z = jnp.where(shared_z, 0.5, 1.0).astype(F32)
    low_y = jnp.where(y > 0, 0.5, 1.0).astype(F32)
    high_y = jnp.where(y < ny - 1, 0.5, 1.0).astype(F32)
    low_x = jnp.where(x > 0, 0.5, 1.0).astype(F32)
    high_x = jnp.where(x < nx - 1, 0.5, 1.0).astype(F32)
    weight_yz = weight_z * jnp.where(row < N, low_y, jnp.where(row >= N * N - N, high_y, 1.0))

    def from_below(v):
        return jnp.where(lane > 0, pltpu.roll(v, 1, axis=1), 0.0)

    def from_above(v):
        return jnp.where(lane < last, pltpu.roll(v, last, axis=1), 0.0)

    def total(v):
        return jnp.sum(jnp.sum(v, axis=0, keepdims=True), axis=1, keepdims=True)

    def weighted(product):
        middle = product(1)
        for a in range(2, N - 1):
            middle = middle + product(a)
        return total(weight_yz * (low_x * product(0) + middle + high_x * product(N - 1)))

    own = pl.ds(N, N * N)

    def stage(buffer, index, send, recv, count, device):
        def copy(k):
            return pltpu.make_async_remote_copy(
                src_ref=buffer.at[pl.ds(index, 1)],
                dst_ref=buffer.at[pl.ds(index, 1)],
                send_sem=send,
                recv_sem=recv,
                device_id=device(k),
                device_id_type=MESH,
            )

        @pl.loop(1, count)
        def _(k):
            copy(k).start()

    def all_rows(buffer, send, recv, count):
        rows = buffer.at[pl.ds(0, count - 1)]
        pltpu.make_async_copy(rows, rows, recv).wait()
        pltpu.make_async_copy(rows, rows, send).wait()

    def gather_y(g, value):
        buf_y[g, pl.ds(y, 1)] = value.reshape(1, 1, 128)
        stage(buf_y.at[g], y, gy_send.at[g], gy_recv.at[g], ny, lambda k: (x, lax.rem(y + k, ny)))

    def gather_x(g):
        all_rows(buf_y.at[g], gy_send.at[g], gy_recv.at[g], ny)
        value = jnp.sum(buf_y[g].reshape(ny, 128) * along_y[...], axis=0, keepdims=True)
        buf_x[g, pl.ds(x, 1)] = value.reshape(1, 1, 128)
        stage(buf_x.at[g], x, gx_send.at[g], gx_recv.at[g], nx, lambda k: (lax.rem(x + k, nx), y))

    def gathered(g):
        all_rows(buf_x.at[g], gx_send.at[g], gx_recv.at[g], nx)
        value = jnp.sum(buf_x[g].reshape(nx, 128) * along_x[...], axis=0, keepdims=True)
        sums = jnp.sum(value * back[...], axis=1, keepdims=True)
        sv[g] = jnp.broadcast_to(sums, (16, 128))

    def lifted(g):
        for t in range(3):
            for s in range(3):
                at, count = ((0, 1), (1, N - 2), (N - 1, 1))[s]
                lift[t, pl.ds(at * N, count * N)] = jnp.broadcast_to(sv[g, pl.ds(3 * t + s, 1)], (count * N, 128))

    def message(*values):
        result = values[0]
        for i, value in enumerate(values[1:]):
            result = jnp.where(lane < PLAIN + 16 * i, result, value)
        return jnp.broadcast_to(result, (1, 128))

    def product(matrix, v):
        high = v.astype(BF16)
        low = (v - high.astype(F32)).astype(BF16)
        out = jnp.dot(matrix, jnp.concatenate([high, low], axis=1), preferred_element_type=F32)
        half = matrix.shape[0] // 2
        return (out[half:, :128] + out[:half, 128:]) + out[:half, :128]

    def solve(ext, loc):
        h = (N + 2) // 2
        for i in range(h):
            lower, upper = ext[i], ext[N + 1 - i]
            even, odd = lower + upper, lower - upper
            for j in range(h):
                one, two = slice(j * N, j * N + N), slice((N + 1 - j) * N, (N + 2 - j) * N)
                at = pl.ds((i * h + j) * N, N)
                blk[0, at] = even[one] + even[two]
                blk[1, at] = even[one] - even[two]
                blk[2, at] = odd[one] + odd[two]
                blk[3, at] = odd[one] - odd[two]
        count = h * h

        @pl.loop(0, 4)
        def _(p):
            source, out = blk.at[p], oblk.at[p]
            below = source[pl.ds(N - 2, count, stride=N)]
            above = source[pl.ds(1, count, stride=N)]
            source[pl.ds(count * N, count)] = from_below(below)
            source[pl.ds(count * (N + 1), count)] = from_above(above)
            out[...] = product(schwarz[p], source[...])
            first = out[pl.ds(0, count, stride=N)]
            final = out[pl.ds(N - 1, count, stride=N)]
            out[pl.ds(0, count, stride=N)] = first + from_below(final)
            out[pl.ds(N - 1, count, stride=N)] = final + from_above(first)
            out[pl.ds(1, count, stride=N)] += from_below(out[pl.ds(count * (N + 1), count)])
            out[pl.ds(N - 2, count, stride=N)] += from_above(out[pl.ds(count * N, count)])

        for i in range(h):
            for j in range(h):
                at = pl.ds((i * h + j) * N, N)
                ee, eo, oe, oo = oblk[0, at], oblk[1, at], oblk[2, at], oblk[3, at]
                one, two = pl.ds(j * N, N), pl.ds((N + 1 - j) * N, N)
                loc[i, one] = (ee + eo) + (oe + oo)
                loc[N + 1 - i, one] = (ee + eo) - (oe + oo)
                loc[i, two] = (ee - eo) + (oe - oo)
                loc[N + 1 - i, two] = (ee - eo) - (oe - oo)

    def spread_copies(phase, slot, loc):
        return copies(
            phase,
            lambda dx, dy: loc.at[
                span(*part(dx, (0, 2), (N, 2), (1, N))), span(*part(dy, (0, 2), (N, 2), (1, N)), N)
            ],
            lambda m: incoming(sides, corners, slot, m),
        )

    def add_nodes(field, slot):
        for m, (dx, dy) in enumerate(MOVES):
            area = field.at[
                span(*part(dx, (N - 2, 2), (0, 2), (0, N))), span(*part(dy, (N - 2, 2), (0, 2), (0, N)), N)
            ]
            area[...] += incoming(sides, corners, slot, m)[...]

    def combine(field, loc):
        for a in range(N):
            field[a] = loc[a + 1, own] + lift[0 if a == 0 else (2 if a == N - 1 else 1)]

    porosity = None

    def apply(field, image):
        for a in range(N // 2):
            lower, upper = field[a], field[N - 1 - a]
            ab[0, pl.ds(a * N * N, N * N)] = lower + upper
            ab[1, pl.ds(a * N * N, N * N)] = lower - upper
        even = product(stiff[0], ab[0])
        odd = product(stiff[1], ab[1])
        for a in range(N // 2):
            at = slice(a * N * N, (a + 1) * N * N)
            scaled = mass[...] * F32(node_weights[a])
            image[a] = porosity * (even[at] + odd[at]) + scaled * field[a]
            image[N - 1 - a] = porosity * (even[at] - odd[at]) + scaled * field[N - 1 - a]
        for a in range(N):
            first = image[a, pl.ds(0, N, stride=N)]
            final = image[a, pl.ds(N - 1, N, stride=N)]
            image[a, pl.ds(0, N, stride=N)] = first + from_below(final)
            image[a, pl.ds(N - 1, N, stride=N)] = final + from_above(first)

    loads[0].wait()
    coarse0 = weighted(lambda a: ext0[a + 1, own])
    gather_y(0, message(coarse0))
    for p in range(4):
        blk[p, pl.ds(248, 8)] = jnp.zeros((8, 128), F32)
    for load in loads[1:]:
        load.wait()
    porosity = 1.0 - 0.6 * grains[...].astype(F32) / MOST_GRAINS
    gather_x(0)
    arrive(halo0)
    solve(ext0, loc0)
    spread0 = spread_copies(1, 0, loc0)
    start(spread0)
    gathered(0)
    lifted(0)
    combine(d, loc0)
    arrive(spread0)
    add_nodes(d, 0)

    apply(d, q1)
    faces = copies(
        2,
        lambda dx, dy: q1.at[
            span(*part(dx, (0, 2), (N - 2, 2), (0, N))), span(*part(dy, (0, 2), (N - 2, 2), (0, N)), N)
        ],
        lambda m: incoming(sides, corners, 1, m),
    )
    start(faces)
    rho1 = weighted(lambda a: ext0[a + 1, own] * d[a])
    curve = d[0] * q1[0]
    for a in range(1, N):
        curve = curve + d[a] * q1[a]
    curve1 = total(weight_z * curve)
    for i in (0, N + 1):
        ext1[i] = jnp.zeros_like(ext1[i])
    for a in range(N):
        ext1[a + 1, pl.ds(0, N)] = jnp.zeros((N, 128), F32)
        ext1[a + 1, own] = q1[a]
        ext1[a + 1, pl.ds(N * N + N, N)] = jnp.zeros((N, 128), F32)
    arrive(faces)
    for m, (dx, dy) in enumerate(MOVES):
        area = ext1.at[span(*part(dx, (N, 2), (0, 2), (1, N))), span(*part(dy, (N, 2), (0, 2), (1, N)), N)]
        area[...] += incoming(sides, corners, 1, m)[...]

    coarse1 = weighted(lambda a: ext1[a + 1, own])
    gather_y(1, message(coarse1, rho1, curve1))
    solve(ext1, loc1)
    spread1 = spread_copies(3, 2, loc1)
    start(spread1)
    gather_x(1)
    gathered(1)
    lifted(1)
    combine(w, loc1)
    arrive(spread1)
    add_nodes(w, 2)

    apply(w, qw)
    edges = copies(
        4,
        lambda dx, dy: qw.at[
            span(*part(dx, (0, 1), (N - 1, 1), (0, N))), span(*part(dy, (0, 1), (N - 1, 1), (0, N)), N)
        ],
        lambda m: incoming(sides1, corners1, None, m),
    )
    start(edges)
    rho1, curve1 = sv[1, pl.ds(9, 1)], sv[1, pl.ds(10, 1)]
    step1 = rho1 / curve1
    curve_new, curve_mixed = None, None
    for a in range(N):
        z_a = d[a] - step1 * w[a]
        z2[a] = z_a
        r1[a] = ext0[a + 1, own] - step1 * ext1[a + 1, own]
        new = z_a * (q1[a] - step1 * qw[a])
        mixed = z_a * q1[a]
        curve_new = new if a == 0 else curve_new + new
        curve_mixed = mixed if a == 0 else curve_mixed + mixed
    rho2 = weighted(lambda a: r1[a] * z2[a])
    gather_y(2, message(rho2, rho2, total(weight_z * curve_new), total(weight_z * curve_mixed)))
    for a in range(N):
        im2[a] = qw[a]
    arrive(edges)
    for m, (dx, dy) in enumerate(MOVES):
        area = im2.at[
            span(*part(dx, (N - 1, 1), (0, 1), (0, N))), span(*part(dy, (N - 1, 1), (0, 1), (0, N)), N)
        ]
        area[...] += incoming(sides1, corners1, None, m)[...]
    gather_x(2)
    for a in range(N):
        im2[a] = ext1[a + 1, own] - step1 * im2[a]
        sol[a] = sol[a] + step1 * d[a]
    gathered(2)
    rho2, curve_new, curve_mixed = sv[2, pl.ds(9, 1)], sv[2, pl.ds(10, 1)], sv[2, pl.ds(11, 1)]
    ratio = rho2 / rho1
    step2 = rho2 / (curve_new + ratio * (2.0 * curve_mixed + ratio * curve1))
    for a in range(N):
        direction = z2[a] + ratio * d[a]
        dir_out[0, 0, a] = direction
        sol_out[0, 0, a] = sol[a] + step2 * direction
        res_out[0, 0, a] = r1[a] - step2 * (im2[a] + ratio * ext1[a + 1, own])
    steps_out[0] = step1[0, 0]
    steps_out[1] = step2[0, 0]
    for group in (halo0, spread0, faces, spread1, edges):
        sent(group)


def incoming(sides, corners, slot, m):
    first, second = MOVES[m]
    if first and second:
        return corners.at[m - 4] if slot is None else corners.at[slot, m - 4]
    which = 0 if first else 1
    ref = sides[which]
    return ref.at[m % 2] if slot is None else ref.at[slot, m % 2]


def solution(mesh):
    nx, ny = mesh.shape["gx"], mesh.shape["gy"]
    weights, _ = gll_tables()
    along_y, along_x, back = coarse_tables(nx, ny, 128)
    schwarz, stiff, mass = schwarz_blocks(), stiffness_blocks(), mass_table()
    nn = N * N
    field = pltpu.VMEM((N, nn, 128), F32)
    wide = pltpu.VMEM((N + 2, nn + 2 * N, 128), F32)
    vmem, anywhere = pl.BlockSpec(memory_space=pltpu.VMEM), pl.BlockSpec(memory_space=pl.ANY)
    smem = pl.BlockSpec(memory_space=pltpu.SMEM)

    def step(sol, res, grains):
        shape = sol.shape
        flat = (1, 1, N, nn, 128)
        out = jax.ShapeDtypeStruct(flat, F32)
        outs = pl.pallas_call(
            functools.partial(kernel, nx, ny, [float(v) for v in weights]),
            out_shape=(out, out, out, jax.ShapeDtypeStruct((2,), F32)),
            in_specs=[anywhere] * 9,
            out_specs=(vmem, vmem, vmem, smem),
            scratch_shapes=[
                field, wide, wide,
                pltpu.VMEM((1, 128), jnp.int32),
                pltpu.VMEM((4, 512, 256), BF16),
                pltpu.VMEM((2, 512, 256), BF16),
                pltpu.VMEM((ny, 128), F32),
                pltpu.VMEM((nx, 128), F32),
                pltpu.VMEM((16, 128), F32),
                pltpu.VMEM((nn, 128), F32),
                pltpu.VMEM((4, 256, 128), F32),
                pltpu.VMEM((4, 256, 128), F32),
                pltpu.VMEM((2, 256, 128), F32),
                wide, wide, field, field, field, field,
                pltpu.VMEM((3, nn, 128), F32),
                pltpu.VMEM((8, 128), F32),
                pltpu.VMEM((3, ny, 1, 128), F32),
                pltpu.VMEM((3, nx, 1, 128), F32),
                pltpu.VMEM((3, 16, 128), F32),
                [pltpu.VMEM((3, 2, 2, nn, 128), F32), pltpu.VMEM((3, 2, N, 2 * N, 128), F32)],
                pltpu.VMEM((3, 4, 2, 2 * N, 128), F32),
                [pltpu.VMEM((2, 1, nn, 128), F32), pltpu.VMEM((2, N, N, 128), F32)],
                pltpu.VMEM((4, 1, N, 128), F32),
                field, field, field,
                pltpu.SemaphoreType.DMA((9,)),
                pltpu.SemaphoreType.DMA((5, 8)),
                pltpu.SemaphoreType.DMA((5, 8)),
                pltpu.SemaphoreType.DMA((3,)),
                pltpu.SemaphoreType.DMA((3,)),
                pltpu.SemaphoreType.DMA((3,)),
                pltpu.SemaphoreType.DMA((3,)),
            ],
            compiler_params=pltpu.CompilerParams(
                collective_id=0, has_side_effects=True, vmem_limit_bytes=40 * 1024 * 1024
            ),
            name="cg_steps",
        )(
            sol.reshape(flat), res.reshape(flat), grains,
            jnp.asarray(schwarz), jnp.asarray(stiff), jnp.asarray(along_y), jnp.asarray(along_x),
            jnp.asarray(back), jnp.asarray(mass),
        )
        return tuple(v.reshape(shape) for v in outs[:3]) + (outs[3],)

    wide_spec = P("gx", "gy", None, None, None, None)
    return jax.shard_map(
        step,
        mesh=mesh,
        in_specs=(wide_spec, wide_spec, P("gx", "gy", None)),
        out_specs=(wide_spec, wide_spec, wide_spec, P()),
        check_vma=False,
    )
```

```python
import functools
import math

import jax
import jax.numpy as jnp
import ml_dtypes
import numpy as np
from jax import lax
from jax.experimental import pallas as pl
from jax.experimental.pallas import tpu as pltpu
from jax.sharding import PartitionSpec as P

N = 8
MOST_GRAINS = 16
shift_mass = 0.1
mean_porosity = 0.7
MESH = pl.DeviceIdType.MESH
F32 = jnp.float32
BF16 = jnp.bfloat16
MOVES = [(1, 0), (-1, 0), (0, 1), (0, -1), (1, 1), (1, -1), (-1, 1), (-1, -1)]
LONGEST_FIRST = [4, 5, 6, 7, 0, 1, 2, 3]
PLAIN = 48


def legendre_columns(node_set, degree):
    table = [node_set * 0.0 + 1.0, node_set]
    for order in range(2, degree + 1):
        table.append(((2 * order - 1) * node_set * table[order - 1] - (order - 1) * table[order - 2]) / order)
    return table


def gll_tables():
    degree = N - 1
    node_set = np.cos(math.pi * np.arange(degree + 1) / degree)
    for _ in range(100):
        table = legendre_columns(node_set, degree)
        node_set = node_set - (node_set * table[degree] - table[degree - 1]) / ((degree + 1) * table[degree])
    node_set = node_set[::-1].copy()
    values = legendre_columns(node_set, degree)[degree]
    weights = 2.0 / (degree * (degree + 1) * values**2)
    derivative = np.zeros((N, N))
    for a in range(N):
        for b in range(N):
            if a != b:
                derivative[a, b] = values[a] / (values[b] * (node_set[a] - node_set[b]))
    derivative[0, 0] = -degree * (degree + 1) / 4.0
    derivative[N - 1, N - 1] = degree * (degree + 1) / 4.0
    return weights, derivative


def schwarz_tables():
    weights, derivative = gll_tables()
    stiffness = derivative.T @ (weights[:, None] * derivative)
    total = 3 * (N - 1) + 1
    three_stiffness = np.zeros((total, total))
    three_mass = np.zeros(total)
    for element in range(3):
        at = element * (N - 1)
        three_stiffness[at : at + N, at : at + N] += stiffness
        three_mass[at : at + N] += weights
    chosen = np.array([N - 2] + list(range(N - 1, 2 * N - 1)) + [2 * N - 1])
    scaling = 1.0 / np.sqrt(three_mass[chosen])
    symmetric = scaling[:, None] * three_stiffness[chosen][:, chosen] * scaling[None, :]
    values, vectors = np.linalg.eigh(0.5 * (symmetric + symmetric.T))
    return scaling[:, None] * vectors, values


def hi_lo(matrix):
    high = matrix.astype(ml_dtypes.bfloat16)
    low = (matrix - high.astype(np.float64)).astype(ml_dtypes.bfloat16)
    return np.concatenate([high, low], axis=-2)


def schwarz_blocks():
    basis, values = schwarz_tables()
    m = N + 2
    divisor = mean_porosity * (values[:, None, None] + values[None, :, None] + values[None, None, :]) + shift_mass
    fold = np.zeros((2, m // 2, m))
    for i in range(m // 2):
        fold[0, i, i] = fold[0, i, m - 1 - i] = 1.0
        fold[1, i, i], fold[1, i, m - 1 - i] = 1.0, -1.0
    order = np.zeros((m // 2, m // 2, m), np.int64)
    for i in range(m // 2):
        for j in range(m // 2):
            at = i * (m // 2) + j
            order[i, j, 1 : m - 1] = at * N + np.arange(N)
            order[i, j, 0] = (m // 2) ** 2 * N + at
            order[i, j, m - 1] = (m // 2) ** 2 * (N + 1) + at
    order = order.reshape(-1)
    blocks = np.zeros((4, 256, 256))
    for p in range(2):
        for q in range(2):
            left = np.kron(np.kron(fold[p] @ basis, fold[q] @ basis), basis)
            block = (left / divisor.reshape(-1)) @ left.T / 16.0
            blocks[2 * p + q][np.ix_(order, order)] = block
    return hi_lo(blocks)


def stiffness_blocks():
    weights, derivative = gll_tables()
    one = derivative.T @ (weights[:, None] * derivative)
    mass = np.diag(weights)
    whole = (
        np.kron(np.kron(one, mass), mass) + np.kron(np.kron(mass, one), mass) + np.kron(np.kron(mass, mass), one)
    )
    half = N // 2 * N * N
    blocks = np.zeros((2, half, half))
    for p, sign in enumerate((1.0, -1.0)):
        fold = np.zeros((N // 2, N))
        for i in range(N // 2):
            fold[i, i], fold[i, N - 1 - i] = 1.0, sign
        fold = np.kron(fold, np.eye(N * N))
        blocks[p] = fold @ whole @ fold.T / 4.0
    return hi_lo(blocks)


def cosine_basis(count):
    position = np.arange(count, dtype=np.float64)
    phase = math.pi * (position[:, None] + 0.5) * position[None, :] / count
    norm = np.where(position == 0, math.sqrt(1.0 / count), math.sqrt(2.0 / count))
    return np.cos(phase) * norm[None, :], 2.0 - 2.0 * np.cos(math.pi * position / count)


def share_rows(count):
    table = np.zeros((count, 3, count))
    for at in range(count):
        table[at, :, at] = 1.0
        if at > 0:
            table[at, 0, at], table[at, 0, at - 1] = 0.5, 0.5
        if at < count - 1:
            table[at, 2, at], table[at, 2, at + 1] = 0.5, 0.5
    return table


def coarse_tables(nx, ny, length):
    first, eigen_first = cosine_basis(nx)
    second, eigen_second = cosine_basis(ny)
    divisor = (
        2.0 * mean_porosity * length * (eigen_first[:, None] + eigen_second[None, :]) + 8.0 * shift_mass * length
    )
    share_first, share_second = share_rows(nx), share_rows(ny)
    green = np.einsum("ap,bp,pk->kab", first, first, 1.0 / divisor)
    send = np.zeros((ny, 16, 128))
    back = np.zeros((ny, 16, 128))
    along_x = np.ones((nx, 3, nx, 128))
    for t in range(3):
        lanes = slice(t * ny, (t + 1) * ny)
        for s in range(3):
            modes = share_second[:, s] @ second
            send[:, 3 * t + s, lanes] = modes
            for other in range(3):
                back[:, 3 * other + s, lanes] = modes
        for other in range(3):
            along_x[:, other, :, lanes] = np.einsum("xc,kcd,bd->xbk", share_first[:, other], green, share_first[:, t])
    for row in range(3):
        send[:, 9 + row, PLAIN + 16 * row] = 1.0
        back[:, 9 + row, PLAIN + 16 * row] = 1.0
    return send.astype(np.float32), along_x.astype(np.float32), back.astype(np.float32)


def mass_table():
    weights, _ = gll_tables()
    table = shift_mass * (weights[:, None] * weights[None, :]).reshape(N * N, 1)
    return np.broadcast_to(table, (N * N, 128)).astype(np.float32).copy()


def part(step, low, high, whole):
    return low if step < 0 else (high if step > 0 else whole)


def span(first, count, unit=1):
    return pl.ds(first * unit, count * unit)


def kernel(
    nx, ny, node_weights,
    sol_in, res_in, grains_in, schwarz_in, stiff_in, send_in, along_x_in, back_in, mass_in,
    sol_out, res_out, dir_out, steps_out,
    sol, ext0, ext1, grains, schwarz, stiff, send_table, along_x, back, mass,
    blk, oblk, ab, loc0, loc1, d, q1, z2, q2, r1, im2, lift, buf_y, buf_x, sv, sides, corners, sides1, corners1,
    load_sem, send_sem, recv_sem, gy_send, gy_recv, gx_send, gx_recv,
):
    x, y = lax.axis_index("gx"), lax.axis_index("gy")

    def inside(dx, dy):
        checks = []
        if dx > 0:
            checks.append(x < nx - 1)
        if dx < 0:
            checks.append(x > 0)
        if dy > 0:
            checks.append(y < ny - 1)
        if dy < 0:
            checks.append(y > 0)
        return functools.reduce(jnp.logical_and, checks)

    barrier = pltpu.get_barrier_semaphore()

    @pl.loop(1, ny)
    def _(k):
        pl.semaphore_signal(barrier, inc=1, device_id=(x, lax.rem(y + k, ny)), device_id_type=MESH)

    @pl.loop(1, nx)
    def _(k):
        pl.semaphore_signal(barrier, inc=1, device_id=(lax.rem(x + k, nx), y), device_id_type=MESH)

    expected = jnp.int32(nx - 1 + ny - 1)
    for dx, dy in MOVES:
        if dx and dy:
            there = inside(dx, dy)
            expected = expected + there.astype(jnp.int32)

            @pl.when(there)
            def _():
                pl.semaphore_signal(barrier, inc=1, device_id=(x + dx, y + dy), device_id_type=MESH)

    loads = [
        pltpu.make_async_copy(src, dst, load_sem.at[i])
        for i, (src, dst) in enumerate(
            [
                (res_in.at[0, 0], ext0.at[pl.ds(1, N), pl.ds(N, N * N)]),
                (schwarz_in, schwarz),
                (send_in.at[y], send_table),
                (along_x_in.at[x], along_x),
                (back_in.at[y], back),
                (grains_in.at[0], grains),
                (stiff_in, stiff),
                (mass_in, mass),
                (sol_in.at[0, 0], sol),
            ]
        )
    ]
    for load in loads:
        load.start()

    for m, (dx, dy) in enumerate(MOVES):

        @pl.when(jnp.logical_not(inside(-dx, -dy)))
        def _():
            for phase in range(3):
                incoming(sides, corners, phase, m)[...] = jnp.zeros_like(incoming(sides, corners, phase, m))
            edge = incoming(sides1, corners1, None, m)
            edge[...] = jnp.zeros_like(edge)
            area = ext0.at[span(*part(dx, (N + 1, 1), (0, 1), (1, N))), span(*part(dy, (N + 1, 1), (0, 1), (1, N)), N)]
            area[...] = jnp.zeros_like(area)

    lane = lax.broadcasted_iota(jnp.int32, (1, 128), 1)
    last = 127
    row = lax.broadcasted_iota(jnp.int32, (N * N, 128), 0)
    wide = lax.broadcasted_iota(jnp.int32, (N * N, 128), 1)
    inner = lax.rem(row, N)
    shared_z = ((inner == 0) & (wide > 0)) | ((inner == N - 1) & (wide < last))
    weight_z = jnp.where(shared_z, 0.5, 1.0).astype(F32)
    low_y = jnp.where(y > 0, 0.5, 1.0).astype(F32)
    high_y = jnp.where(y < ny - 1, 0.5, 1.0).astype(F32)
    low_x = jnp.where(x > 0, 0.5, 1.0).astype(F32)
    high_x = jnp.where(x < nx - 1, 0.5, 1.0).astype(F32)
    weight_yz = weight_z * jnp.where(row < N, low_y, jnp.where(row >= N * N - N, high_y, 1.0))

    def from_below(v):
        return jnp.where(lane > 0, pltpu.roll(v, 1, axis=1), 0.0)

    def from_above(v):
        return jnp.where(lane < last, pltpu.roll(v, last, axis=1), 0.0)

    def total(v):
        return jnp.sum(jnp.sum(v, axis=0, keepdims=True), axis=1, keepdims=True)

    def weighted(product):
        middle = product(1)
        for a in range(2, N - 1):
            middle = middle + product(a)
        return weight_yz * (low_x * product(0) + middle + high_x * product(N - 1))

    own = pl.ds(N, N * N)

    def classes(field, weight, ends):
        middle = field(1)
        for a in range(2, N - 1):
            middle = middle + field(a)
        rows = []
        for scale, value in zip(ends, (field(0), middle, field(N - 1))):
            value = value * weight * scale
            inner_rows = value[N : 2 * N]
            for b in range(2, N - 1):
                inner_rows = inner_rows + value[b * N : b * N + N]
            for part_rows in (value[:N], inner_rows, value[N * N - N :]):
                rows.append(jnp.sum(part_rows, axis=0, keepdims=True))
        return rows

    def message(rows, *sums):
        result = jnp.zeros((1, 128), F32)
        for i, value in enumerate(rows):
            result = result + jnp.sum(value, axis=1, keepdims=True) * send_table[pl.ds(i, 1)]
        for i, value in enumerate(sums):
            result = result + total(value) * send_table[pl.ds(9 + i, 1)]
        return result

    loads[0].wait()
    loads[2].wait()
    first_message = message(classes(lambda a: ext0[a + 1, own], weight_yz, (low_x, 1.0, high_x)))
    pl.semaphore_wait(barrier, expected)

    def copies(phase, source, target):
        return [
            pltpu.make_async_remote_copy(
                src_ref=source(dx, dy),
                dst_ref=target(m),
                send_sem=send_sem.at[phase, m],
                recv_sem=recv_sem.at[phase, m],
                device_id=(x + dx, y + dy),
                device_id_type=MESH,
            )
            for m, (dx, dy) in enumerate(MOVES)
        ]

    def start(group):
        for m in LONGEST_FIRST:
            pl.when(inside(*MOVES[m]))(group[m].start)

    def arrive(group):
        for m, (dx, dy) in enumerate(MOVES):
            pl.when(inside(-dx, -dy))(group[m].wait_recv)

    def sent(group):
        for m, (dx, dy) in enumerate(MOVES):
            pl.when(inside(dx, dy))(group[m].wait_send)

    def ext_target(m):
        dx, dy = MOVES[m]
        return ext0.at[span(*part(dx, (N + 1, 1), (0, 1), (1, N))), span(*part(dy, (N + 1, 1), (0, 1), (1, N)), N)]

    halo0 = copies(
        0,
        lambda dx, dy: res_in.at[
            0, 0, span(*part(dx, (1, 1), (N - 2, 1), (0, N))), span(*part(dy, (1, 1), (N - 2, 1), (0, N)), N)
        ],
        ext_target,
    )

    def stage(buffer, index, send, recv, count, device):
        def copy(k):
            return pltpu.make_async_remote_copy(
                src_ref=buffer.at[pl.ds(index, 1)],
                dst_ref=buffer.at[pl.ds(index, 1)],
                send_sem=send,
                recv_sem=recv,
                device_id=device(k),
                device_id_type=MESH,
            )

        @pl.loop(1, count)
        def _(k):
            copy(k).start()

    def all_rows(buffer, send, recv, count):
        rows = buffer.at[pl.ds(0, count - 1)]
        pltpu.make_async_copy(rows, rows, recv).wait()
        pltpu.make_async_copy(rows, rows, send).wait()

    def gather_y(g, value):
        buf_y[g, pl.ds(y, 1)] = value.reshape(1, 1, 128)
        stage(buf_y.at[g], y, gy_send.at[g], gy_recv.at[g], ny, lambda k: (x, lax.rem(y + k, ny)))

    def gather_x(g):
        all_rows(buf_y.at[g], gy_send.at[g], gy_recv.at[g], ny)
        value = jnp.sum(buf_y[g].reshape(ny, 128), axis=0, keepdims=True)
        buf_x[g, pl.ds(x, 1)] = value.reshape(1, 1, 128)
        stage(buf_x.at[g], x, gx_send.at[g], gx_recv.at[g], nx, lambda k: (lax.rem(x + k, nx), y))

    def gathered(g):
        all_rows(buf_x.at[g], gx_send.at[g], gx_recv.at[g], nx)
        rows = buf_x[g].reshape(nx, 128)
        low, middle, high = (jnp.sum(rows * along_x[t], axis=0, keepdims=True) for t in range(3))
        row16 = lax.broadcasted_iota(jnp.int32, (16, 128), 0)
        value = jnp.where(row16 < 3, low, jnp.where(row16 < 6, middle, high))
        sums = jnp.sum(value * back[...], axis=1, keepdims=True)
        sv[g] = jnp.broadcast_to(sums, (16, 128))

    def lifted(g):
        for t in range(3):
            for s in range(3):
                at, count = ((0, 1), (1, N - 2), (N - 1, 1))[s]
                lift[t, pl.ds(at * N, count * N)] = jnp.broadcast_to(sv[g, pl.ds(3 * t + s, 1)], (count * N, 128))

    def product(matrix, v):
        high = v.astype(BF16)
        low = (v - high.astype(F32)).astype(BF16)
        out = jnp.dot(matrix, jnp.concatenate([high, low], axis=1), preferred_element_type=F32)
        half = matrix.shape[0] // 2
        return (out[half:, :128] + out[:half, 128:]) + out[:half, :128]

    def solve(ext, loc):
        h = (N + 2) // 2
        for i in range(h):
            lower, upper = ext[i], ext[N + 1 - i]
            even, odd = lower + upper, lower - upper
            for j in range(h):
                one, two = slice(j * N, j * N + N), slice((N + 1 - j) * N, (N + 2 - j) * N)
                at = pl.ds((i * h + j) * N, N)
                blk[0, at] = even[one] + even[two]
                blk[1, at] = even[one] - even[two]
                blk[2, at] = odd[one] + odd[two]
                blk[3, at] = odd[one] - odd[two]
        count = h * h

        @pl.loop(0, 4)
        def _(p):
            source, out = blk.at[p], oblk.at[p]
            below = source[pl.ds(N - 2, count, stride=N)]
            above = source[pl.ds(1, count, stride=N)]
            source[pl.ds(count * N, count)] = from_below(below)
            source[pl.ds(count * (N + 1), count)] = from_above(above)
            out[...] = product(schwarz[p], source[...])
            first = out[pl.ds(0, count, stride=N)]
            final = out[pl.ds(N - 1, count, stride=N)]
            out[pl.ds(0, count, stride=N)] = first + from_below(final)
            out[pl.ds(N - 1, count, stride=N)] = final + from_above(first)
            out[pl.ds(1, count, stride=N)] += from_below(out[pl.ds(count * (N + 1), count)])
            out[pl.ds(N - 2, count, stride=N)] += from_above(out[pl.ds(count * N, count)])

        for i in range(h):
            for j in range(h):
                at = pl.ds((i * h + j) * N, N)
                ee, eo, oe, oo = oblk[0, at], oblk[1, at], oblk[2, at], oblk[3, at]
                one, two = pl.ds(j * N, N), pl.ds((N + 1 - j) * N, N)
                loc[i, one] = (ee + eo) + (oe + oo)
                loc[N + 1 - i, one] = (ee + eo) - (oe + oo)
                loc[i, two] = (ee - eo) + (oe - oo)
                loc[N + 1 - i, two] = (ee - eo) - (oe - oo)

    def spread_copies(phase, slot, loc):
        return copies(
            phase,
            lambda dx, dy: loc.at[
                span(*part(dx, (0, 2), (N, 2), (1, N))), span(*part(dy, (0, 2), (N, 2), (1, N)), N)
            ],
            lambda m: incoming(sides, corners, slot, m),
        )

    def node_area(field, dx, dy):
        return field.at[span(*part(dx, (N - 2, 2), (0, 2), (0, N))), span(*part(dy, (N - 2, 2), (0, 2), (0, N)), N)]

    porosity = None

    def apply(field, image):
        for a in range(N // 2):
            lower, upper = field[a], field[N - 1 - a]
            ab[0, pl.ds(a * N * N, N * N)] = lower + upper
            ab[1, pl.ds(a * N * N, N * N)] = lower - upper
        even = product(stiff[0], ab[0])
        odd = product(stiff[1], ab[1])
        for a in range(N // 2):
            at = slice(a * N * N, (a + 1) * N * N)
            scaled = mass[...] * F32(node_weights[a])
            image[a] = porosity * (even[at] + odd[at]) + scaled * field[a]
            image[N - 1 - a] = porosity * (even[at] - odd[at]) + scaled * field[N - 1 - a]
        for a in range(N):
            first = image[a, pl.ds(0, N, stride=N)]
            final = image[a, pl.ds(N - 1, N, stride=N)]
            image[a, pl.ds(0, N, stride=N)] = first + from_below(final)
            image[a, pl.ds(N - 1, N, stride=N)] = final + from_above(first)

    gather_y(0, first_message)
    start(halo0)
    for p in range(4):
        blk[p, pl.ds(248, 8)] = jnp.zeros((8, 128), F32)
    for i, load in enumerate(loads):
        if i not in (0, 2):
            load.wait()
    porosity = 1.0 - 0.6 * grains[...].astype(F32) / MOST_GRAINS
    gather_x(0)
    arrive(halo0)
    solve(ext0, loc0)
    spread0 = spread_copies(1, 0, loc0)
    start(spread0)
    gathered(0)
    lifted(0)
    for a in range(N):
        d[a] = loc0[a + 1, own] + lift[0 if a == 0 else (2 if a == N - 1 else 1)]
    arrive(spread0)
    for m, (dx, dy) in enumerate(MOVES):
        area = node_area(d, dx, dy)
        area[...] += incoming(sides, corners, 0, m)[...]

    apply(d, q1)
    rho1 = weighted(lambda a: ext0[a + 1, own] * d[a])
    curve = d[0] * q1[0]
    for a in range(1, N):
        curve = curve + d[a] * q1[a]
    gather_y(1, message(classes(lambda a: q1[a], weight_z, (1.0, 1.0, 1.0)), rho1, weight_z * curve))
    faces = copies(
        2,
        lambda dx, dy: q1.at[
            span(*part(dx, (0, 2), (N - 2, 2), (0, N))), span(*part(dy, (0, 2), (N - 2, 2), (0, N)), N)
        ],
        lambda m: incoming(sides, corners, 1, m),
    )
    start(faces)
    for i in (0, N + 1):
        ext1[i] = jnp.zeros_like(ext1[i])
    for a in range(N):
        ext1[a + 1, pl.ds(0, N)] = jnp.zeros((N, 128), F32)
        ext1[a + 1, own] = q1[a]
        ext1[a + 1, pl.ds(N * N + N, N)] = jnp.zeros((N, 128), F32)
    gather_x(1)
    arrive(faces)
    for m, (dx, dy) in enumerate(MOVES):
        area = ext1.at[span(*part(dx, (N, 2), (0, 2), (1, N))), span(*part(dy, (N, 2), (0, 2), (1, N)), N)]
        area[...] += incoming(sides, corners, 1, m)[...]

    solve(ext1, loc1)
    spread1 = spread_copies(3, 2, loc1)
    start(spread1)
    gathered(1)
    lifted(1)
    rho1, curve1 = sv[1, pl.ds(9, 1)], sv[1, pl.ds(10, 1)]
    step1 = rho1 / curve1
    for a in range(N):
        z2[a] = d[a] - step1 * (loc1[a + 1, own] + lift[0 if a == 0 else (2 if a == N - 1 else 1)])
        r1[a] = ext0[a + 1, own] - step1 * ext1[a + 1, own]
        sol[a] = sol[a] + step1 * d[a]
    arrive(spread1)
    for m, (dx, dy) in enumerate(MOVES):
        area = node_area(z2, dx, dy)
        area[...] -= step1 * incoming(sides, corners, 2, m)[...]

    apply(z2, q2)
    curve_new = z2[0] * q2[0]
    curve_mixed = z2[0] * q1[0]
    for a in range(1, N):
        curve_new = curve_new + z2[a] * q2[a]
        curve_mixed = curve_mixed + z2[a] * q1[a]
    rho2 = weighted(lambda a: r1[a] * z2[a])
    gather_y(2, message([], rho2, weight_z * curve_new, weight_z * curve_mixed))
    edges = copies(
        4,
        lambda dx, dy: q2.at[
            span(*part(dx, (0, 1), (N - 1, 1), (0, N))), span(*part(dy, (0, 1), (N - 1, 1), (0, N)), N)
        ],
        lambda m: incoming(sides1, corners1, None, m),
    )
    start(edges)
    for a in range(N):
        im2[a] = q2[a]
    gather_x(2)
    arrive(edges)
    for m, (dx, dy) in enumerate(MOVES):
        area = im2.at[
            span(*part(dx, (N - 1, 1), (0, 1), (0, N))), span(*part(dy, (N - 1, 1), (0, 1), (0, N)), N)
        ]
        area[...] += incoming(sides1, corners1, None, m)[...]
    for group in (halo0, spread0, faces, spread1, edges):
        sent(group)
    gathered(2)
    rho2, curve_new, curve_mixed = sv[2, pl.ds(9, 1)], sv[2, pl.ds(10, 1)], sv[2, pl.ds(11, 1)]
    ratio = rho2 / rho1
    step2 = rho2 / (curve_new + ratio * (2.0 * curve_mixed + ratio * curve1))
    for a in range(N):
        direction = z2[a] + ratio * d[a]
        dir_out[0, 0, a] = direction
        sol_out[0, 0, a] = sol[a] + step2 * direction
        res_out[0, 0, a] = r1[a] - step2 * (im2[a] + ratio * ext1[a + 1, own])
    steps_out[0] = step1[0, 0]
    steps_out[1] = step2[0, 0]


def incoming(sides, corners, slot, m):
    first, second = MOVES[m]
    if first and second:
        return corners.at[m - 4] if slot is None else corners.at[slot, m - 4]
    which = 0 if first else 1
    ref = sides[which]
    return ref.at[m % 2] if slot is None else ref.at[slot, m % 2]


def solution(mesh):
    nx, ny = mesh.shape["gx"], mesh.shape["gy"]
    weights, _ = gll_tables()
    send, along_x, back = coarse_tables(nx, ny, 128)
    schwarz, stiff, mass = schwarz_blocks(), stiffness_blocks(), mass_table()
    nn = N * N
    field = pltpu.VMEM((N, nn, 128), F32)
    wide = pltpu.VMEM((N + 2, nn + 2 * N, 128), F32)
    vmem, anywhere = pl.BlockSpec(memory_space=pltpu.VMEM), pl.BlockSpec(memory_space=pl.ANY)
    smem = pl.BlockSpec(memory_space=pltpu.SMEM)

    def step(sol, res, grains):
        shape = sol.shape
        flat = (1, 1, N, nn, 128)
        out = jax.ShapeDtypeStruct(flat, F32)
        outs = pl.pallas_call(
            functools.partial(kernel, nx, ny, [float(v) for v in weights]),
            out_shape=(out, out, out, jax.ShapeDtypeStruct((2,), F32)),
            in_specs=[anywhere] * 9,
            out_specs=(vmem, vmem, vmem, smem),
            scratch_shapes=[
                field, wide, wide,
                pltpu.VMEM((1, 128), jnp.int32),
                pltpu.VMEM((4, 512, 256), BF16),
                pltpu.VMEM((2, 512, 256), BF16),
                pltpu.VMEM((16, 128), F32),
                pltpu.VMEM((3, nx, 128), F32),
                pltpu.VMEM((16, 128), F32),
                pltpu.VMEM((nn, 128), F32),
                pltpu.VMEM((4, 256, 128), F32),
                pltpu.VMEM((4, 256, 128), F32),
                pltpu.VMEM((2, 256, 128), F32),
                wide, wide, field, field, field, field, field, field,
                pltpu.VMEM((3, nn, 128), F32),
                pltpu.VMEM((3, ny, 1, 128), F32),
                pltpu.VMEM((3, nx, 1, 128), F32),
                pltpu.VMEM((3, 16, 128), F32),
                [pltpu.VMEM((3, 2, 2, nn, 128), F32), pltpu.VMEM((3, 2, N, 2 * N, 128), F32)],
                pltpu.VMEM((3, 4, 2, 2 * N, 128), F32),
                [pltpu.VMEM((2, 1, nn, 128), F32), pltpu.VMEM((2, N, N, 128), F32)],
                pltpu.VMEM((4, 1, N, 128), F32),
                pltpu.SemaphoreType.DMA((9,)),
                pltpu.SemaphoreType.DMA((5, 8)),
                pltpu.SemaphoreType.DMA((5, 8)),
                pltpu.SemaphoreType.DMA((3,)),
                pltpu.SemaphoreType.DMA((3,)),
                pltpu.SemaphoreType.DMA((3,)),
                pltpu.SemaphoreType.DMA((3,)),
            ],
            compiler_params=pltpu.CompilerParams(collective_id=0, has_side_effects=True),
            name="cg_steps",
        )(
            sol.reshape(flat), res.reshape(flat), grains,
            jnp.asarray(schwarz), jnp.asarray(stiff), jnp.asarray(send), jnp.asarray(along_x),
            jnp.asarray(back), jnp.asarray(mass),
        )
        return tuple(v.reshape(shape) for v in outs[:3]) + (outs[3],)

    wide_spec = P("gx", "gy", None, None, None, None)
    return jax.shard_map(
        step,
        mesh=mesh,
        in_specs=(wide_spec, wide_spec, P("gx", "gy", None)),
        out_specs=(wide_spec, wide_spec, wide_spec, P()),
        check_vma=False,
    )
```

```python
import functools
import math

import jax
import jax.numpy as jnp
import ml_dtypes
import numpy as np
from jax import lax
from jax.experimental import pallas as pl
from jax.experimental.pallas import tpu as pltpu
from jax.sharding import PartitionSpec as P

N = 8
MOST_GRAINS = 16
shift_mass = 0.1
mean_porosity = 0.7
MESH = pl.DeviceIdType.MESH
F32 = jnp.float32
BF16 = jnp.bfloat16
MOVES = [(1, 0), (-1, 0), (0, 1), (0, -1), (1, 1), (1, -1), (-1, 1), (-1, -1)]
LONGEST_FIRST = [4, 5, 6, 7, 0, 1, 2, 3]
PLAIN = 48


def legendre_columns(node_set, degree):
    table = [node_set * 0.0 + 1.0, node_set]
    for order in range(2, degree + 1):
        table.append(((2 * order - 1) * node_set * table[order - 1] - (order - 1) * table[order - 2]) / order)
    return table


def gll_tables():
    degree = N - 1
    node_set = np.cos(math.pi * np.arange(degree + 1) / degree)
    for _ in range(100):
        table = legendre_columns(node_set, degree)
        node_set = node_set - (node_set * table[degree] - table[degree - 1]) / ((degree + 1) * table[degree])
    node_set = node_set[::-1].copy()
    values = legendre_columns(node_set, degree)[degree]
    weights = 2.0 / (degree * (degree + 1) * values**2)
    derivative = np.zeros((N, N))
    for a in range(N):
        for b in range(N):
            if a != b:
                derivative[a, b] = values[a] / (values[b] * (node_set[a] - node_set[b]))
    derivative[0, 0] = -degree * (degree + 1) / 4.0
    derivative[N - 1, N - 1] = degree * (degree + 1) / 4.0
    return weights, derivative


def schwarz_tables():
    weights, derivative = gll_tables()
    stiffness = derivative.T @ (weights[:, None] * derivative)
    total = 3 * (N - 1) + 1
    three_stiffness = np.zeros((total, total))
    three_mass = np.zeros(total)
    for element in range(3):
        at = element * (N - 1)
        three_stiffness[at : at + N, at : at + N] += stiffness
        three_mass[at : at + N] += weights
    chosen = np.array([N - 2] + list(range(N - 1, 2 * N - 1)) + [2 * N - 1])
    scaling = 1.0 / np.sqrt(three_mass[chosen])
    symmetric = scaling[:, None] * three_stiffness[chosen][:, chosen] * scaling[None, :]
    values, vectors = np.linalg.eigh(0.5 * (symmetric + symmetric.T))
    return scaling[:, None] * vectors, values


def hi_lo(matrix):
    high = matrix.astype(ml_dtypes.bfloat16)
    low = (matrix - high.astype(np.float64)).astype(ml_dtypes.bfloat16)
    return np.concatenate([high, low], axis=-2)


def schwarz_blocks():
    basis, values = schwarz_tables()
    m = N + 2
    divisor = mean_porosity * (values[:, None, None] + values[None, :, None] + values[None, None, :]) + shift_mass
    fold = np.zeros((2, m // 2, m))
    for i in range(m // 2):
        fold[0, i, i] = fold[0, i, m - 1 - i] = 1.0
        fold[1, i, i], fold[1, i, m - 1 - i] = 1.0, -1.0
    order = np.zeros((m // 2, m // 2, m), np.int64)
    for i in range(m // 2):
        for j in range(m // 2):
            at = i * (m // 2) + j
            order[i, j, 1 : m - 1] = at * N + np.arange(N)
            order[i, j, 0] = (m // 2) ** 2 * N + at
            order[i, j, m - 1] = (m // 2) ** 2 * (N + 1) + at
    order = order.reshape(-1)
    blocks = np.zeros((4, 256, 256))
    for p in range(2):
        for q in range(2):
            left = np.kron(np.kron(fold[p] @ basis, fold[q] @ basis), basis)
            block = (left / divisor.reshape(-1)) @ left.T / 16.0
            blocks[2 * p + q][np.ix_(order, order)] = block
    return hi_lo(blocks)


def stiffness_blocks():
    weights, derivative = gll_tables()
    one = derivative.T @ (weights[:, None] * derivative)
    mass = np.diag(weights)
    whole = (
        np.kron(np.kron(one, mass), mass) + np.kron(np.kron(mass, one), mass) + np.kron(np.kron(mass, mass), one)
    )
    half = N // 2 * N * N
    blocks = np.zeros((2, half, half))
    for p, sign in enumerate((1.0, -1.0)):
        fold = np.zeros((N // 2, N))
        for i in range(N // 2):
            fold[i, i], fold[i, N - 1 - i] = 1.0, sign
        fold = np.kron(fold, np.eye(N * N))
        blocks[p] = fold @ whole @ fold.T / 4.0
    return hi_lo(blocks)


def cosine_basis(count):
    position = np.arange(count, dtype=np.float64)
    phase = math.pi * (position[:, None] + 0.5) * position[None, :] / count
    norm = np.where(position == 0, math.sqrt(1.0 / count), math.sqrt(2.0 / count))
    return np.cos(phase) * norm[None, :], 2.0 - 2.0 * np.cos(math.pi * position / count)


def share_rows(count):
    table = np.zeros((count, 3, count))
    for at in range(count):
        table[at, :, at] = 1.0
        if at > 0:
            table[at, 0, at], table[at, 0, at - 1] = 0.5, 0.5
        if at < count - 1:
            table[at, 2, at], table[at, 2, at + 1] = 0.5, 0.5
    return table


def coarse_tables(nx, ny, length):
    first, eigen_first = cosine_basis(nx)
    second, eigen_second = cosine_basis(ny)
    divisor = (
        2.0 * mean_porosity * length * (eigen_first[:, None] + eigen_second[None, :]) + 8.0 * shift_mass * length
    )
    share_first, share_second = share_rows(nx), share_rows(ny)
    green = np.einsum("ap,bp,pk->kab", first, first, 1.0 / divisor)
    send = np.zeros((ny, 16, 128))
    back = np.zeros((ny, 16, 128))
    along_x = np.ones((nx, 3, nx, 128))
    for t in range(3):
        lanes = slice(t * ny, (t + 1) * ny)
        for s in range(3):
            modes = share_second[:, s] @ second
            send[:, 3 * t + s, lanes] = modes
            for other in range(3):
                back[:, 3 * other + s, lanes] = modes
        for other in range(3):
            along_x[:, other, :, lanes] = np.einsum("xc,kcd,bd->xbk", share_first[:, other], green, share_first[:, t])
    for row in range(3):
        send[:, 9 + row, PLAIN + 16 * row] = 1.0
        back[:, 9 + row, PLAIN + 16 * row] = 1.0
    return send.astype(np.float32), along_x.astype(np.float32), back.astype(np.float32)


def mass_table():
    weights, _ = gll_tables()
    table = shift_mass * (weights[:, None] * weights[None, :]).reshape(N * N, 1)
    return np.broadcast_to(table, (N * N, 128)).astype(np.float32).copy()


def part(step, low, high, whole):
    return low if step < 0 else (high if step > 0 else whole)


def span(first, count, unit=1):
    return pl.ds(first * unit, count * unit)


def kernel(
    nx, ny, node_weights,
    sol_in, res_in, grains_in, schwarz_in, stiff_in, send_in, along_x_in, back_in, mass_in,
    sol_out, res_out, dir_out, steps_out,
    sol, ext0, ext1, grains, schwarz, stiff, send_table, along_x, back, mass,
    blk, oblk, ab, loc0, loc1, d, q1, z2, q2, r1, im2, lift, buf_y, buf_x, sv, sides, corners, sides1, corners1,
    load_sem, send_sem, recv_sem, gy_send, gy_recv, gx_send, gx_recv,
):
    x, y = lax.axis_index("gx"), lax.axis_index("gy")

    def inside(dx, dy):
        checks = []
        if dx > 0:
            checks.append(x < nx - 1)
        if dx < 0:
            checks.append(x > 0)
        if dy > 0:
            checks.append(y < ny - 1)
        if dy < 0:
            checks.append(y > 0)
        return functools.reduce(jnp.logical_and, checks)

    barrier = pltpu.get_barrier_semaphore()

    expected = jnp.int32(nx - 1 + ny - 1)
    for dx, dy in MOVES:
        there = inside(dx, dy)
        if dx and dy:
            expected = expected + there.astype(jnp.int32)

        @pl.when(there)
        def _():
            pl.semaphore_signal(barrier, inc=1, device_id=(x + dx, y + dy), device_id_type=MESH)

    @pl.loop(0, nx)
    def _(k):
        @pl.when((k > x + 1) | (k < x - 1))
        def _():
            pl.semaphore_signal(barrier, inc=1, device_id=(k, y), device_id_type=MESH)

    @pl.loop(0, ny)
    def _(k):
        @pl.when((k > y + 1) | (k < y - 1))
        def _():
            pl.semaphore_signal(barrier, inc=1, device_id=(x, k), device_id_type=MESH)

    loads = [
        pltpu.make_async_copy(src, dst, load_sem.at[i])
        for i, (src, dst) in enumerate(
            [
                (res_in.at[0, 0], ext0.at[pl.ds(1, N), pl.ds(N, N * N)]),
                (schwarz_in, schwarz),
                (send_in.at[y], send_table),
                (along_x_in.at[x], along_x),
                (back_in.at[y], back),
                (grains_in.at[0], grains),
                (stiff_in, stiff),
                (mass_in, mass),
                (sol_in.at[0, 0], sol),
            ]
        )
    ]
    for load in loads:
        load.start()

    for m, (dx, dy) in enumerate(MOVES):

        @pl.when(jnp.logical_not(inside(-dx, -dy)))
        def _():
            for phase in range(3):
                incoming(sides, corners, phase, m)[...] = jnp.zeros_like(incoming(sides, corners, phase, m))
            edge = incoming(sides1, corners1, None, m)
            edge[...] = jnp.zeros_like(edge)
            area = ext0.at[span(*part(dx, (N + 1, 1), (0, 1), (1, N))), span(*part(dy, (N + 1, 1), (0, 1), (1, N)), N)]
            area[...] = jnp.zeros_like(area)

    lane = lax.broadcasted_iota(jnp.int32, (1, 128), 1)
    last = 127
    row = lax.broadcasted_iota(jnp.int32, (N * N, 128), 0)
    wide = lax.broadcasted_iota(jnp.int32, (N * N, 128), 1)
    inner = lax.rem(row, N)
    shared_z = ((inner == 0) & (wide > 0)) | ((inner == N - 1) & (wide < last))
    weight_z = jnp.where(shared_z, 0.5, 1.0).astype(F32)
    low_y = jnp.where(y > 0, 0.5, 1.0).astype(F32)
    high_y = jnp.where(y < ny - 1, 0.5, 1.0).astype(F32)
    low_x = jnp.where(x > 0, 0.5, 1.0).astype(F32)
    high_x = jnp.where(x < nx - 1, 0.5, 1.0).astype(F32)
    weight_yz = weight_z * jnp.where(row < N, low_y, jnp.where(row >= N * N - N, high_y, 1.0))

    def from_below(v):
        return jnp.where(lane > 0, pltpu.roll(v, 1, axis=1), 0.0)

    def from_above(v):
        return jnp.where(lane < last, pltpu.roll(v, last, axis=1), 0.0)

    def total(v):
        return jnp.sum(jnp.sum(v, axis=0, keepdims=True), axis=1, keepdims=True)

    def weighted(product):
        middle = product(1)
        for a in range(2, N - 1):
            middle = middle + product(a)
        return weight_yz * (low_x * product(0) + middle + high_x * product(N - 1))

    own = pl.ds(N, N * N)

    def classes(field, weight, ends):
        middle = field(1)
        for a in range(2, N - 1):
            middle = middle + field(a)
        rows = []
        for scale, value in zip(ends, (field(0), middle, field(N - 1))):
            value = value * weight * scale
            inner_rows = value[N : 2 * N]
            for b in range(2, N - 1):
                inner_rows = inner_rows + value[b * N : b * N + N]
            for part_rows in (value[:N], inner_rows, value[N * N - N :]):
                rows.append(jnp.sum(part_rows, axis=0, keepdims=True))
        return rows

    def message(rows, *sums):
        result = jnp.zeros((1, 128), F32)
        for i, value in enumerate(rows):
            result = result + jnp.sum(value, axis=1, keepdims=True) * send_table[pl.ds(i, 1)]
        for i, value in enumerate(sums):
            result = result + total(value) * send_table[pl.ds(9 + i, 1)]
        return result

    pl.semaphore_wait(barrier, expected)

    def copies(phase, source, target):
        return [
            pltpu.make_async_remote_copy(
                src_ref=source(dx, dy),
                dst_ref=target(m),
                send_sem=send_sem.at[phase, m],
                recv_sem=recv_sem.at[phase, m],
                device_id=(x + dx, y + dy),
                device_id_type=MESH,
            )
            for m, (dx, dy) in enumerate(MOVES)
        ]

    def start(group, moves=LONGEST_FIRST):
        for m in moves:
            pl.when(inside(*MOVES[m]))(group[m].start)

    def arrive(group):
        for m, (dx, dy) in enumerate(MOVES):
            pl.when(inside(-dx, -dy))(group[m].wait_recv)

    def sent(group):
        for m, (dx, dy) in enumerate(MOVES):
            pl.when(inside(dx, dy))(group[m].wait_send)

    def ext_target(m):
        dx, dy = MOVES[m]
        return ext0.at[span(*part(dx, (N + 1, 1), (0, 1), (1, N))), span(*part(dy, (N + 1, 1), (0, 1), (1, N)), N)]

    halo0 = copies(
        0,
        lambda dx, dy: res_in.at[
            0, 0, span(*part(dx, (1, 1), (N - 2, 1), (0, N))), span(*part(dy, (1, 1), (N - 2, 1), (0, N)), N)
        ],
        ext_target,
    )

    def stage(buffer, index, send, recv, count, device):
        def copy(k):
            return pltpu.make_async_remote_copy(
                src_ref=buffer.at[pl.ds(index, 1)],
                dst_ref=buffer.at[pl.ds(index, 1)],
                send_sem=send,
                recv_sem=recv,
                device_id=device(k),
                device_id_type=MESH,
            )

        @pl.loop(1, count)
        def _(k):
            copy(k).start()

    def all_rows(buffer, send, recv, count):
        rows = buffer.at[pl.ds(0, count - 1)]
        pltpu.make_async_copy(rows, rows, recv).wait()
        pltpu.make_async_copy(rows, rows, send).wait()

    def gather_y(g, value):
        buf_y[g, pl.ds(y, 1)] = value.reshape(1, 1, 128)
        stage(buf_y.at[g], y, gy_send.at[g], gy_recv.at[g], ny, lambda k: (x, lax.rem(y + k, ny)))

    def gather_x(g):
        all_rows(buf_y.at[g], gy_send.at[g], gy_recv.at[g], ny)
        value = jnp.sum(buf_y[g].reshape(ny, 128), axis=0, keepdims=True)
        buf_x[g, pl.ds(x, 1)] = value.reshape(1, 1, 128)
        stage(buf_x.at[g], x, gx_send.at[g], gx_recv.at[g], nx, lambda k: (lax.rem(x + k, nx), y))

    def gathered(g):
        all_rows(buf_x.at[g], gx_send.at[g], gx_recv.at[g], nx)
        rows = buf_x[g].reshape(nx, 128)
        low, middle, high = (jnp.sum(rows * along_x[t], axis=0, keepdims=True) for t in range(3))
        row16 = lax.broadcasted_iota(jnp.int32, (16, 128), 0)
        value = jnp.where(row16 < 3, low, jnp.where(row16 < 6, middle, high))
        sums = jnp.sum(value * back[...], axis=1, keepdims=True)
        sv[g] = jnp.broadcast_to(sums, (16, 128))

    def lifted(g):
        for t in range(3):
            for s in range(3):
                at, count = ((0, 1), (1, N - 2), (N - 1, 1))[s]
                lift[t, pl.ds(at * N, count * N)] = jnp.broadcast_to(sv[g, pl.ds(3 * t + s, 1)], (count * N, 128))

    def product(matrix, v):
        high = v.astype(BF16)
        low = (v - high.astype(F32)).astype(BF16)
        out = jnp.dot(matrix, jnp.concatenate([high, low], axis=1), preferred_element_type=F32)
        half = matrix.shape[0] // 2
        return (out[half:, :128] + out[:half, 128:]) + out[:half, :128]

    def solve(ext, loc, group):
        h = (N + 2) // 2
        for i in range(h):
            lower, upper = ext[i], ext[N + 1 - i]
            even, odd = lower + upper, lower - upper
            for j in range(h):
                one, two = slice(j * N, j * N + N), slice((N + 1 - j) * N, (N + 2 - j) * N)
                at = pl.ds((i * h + j) * N, N)
                blk[0, at] = even[one] + even[two]
                blk[1, at] = even[one] - even[two]
                blk[2, at] = odd[one] + odd[two]
                blk[3, at] = odd[one] - odd[two]
        count = h * h

        @pl.loop(0, 4)
        def _(p):
            source, out = blk.at[p], oblk.at[p]
            below = source[pl.ds(N - 2, count, stride=N)]
            above = source[pl.ds(1, count, stride=N)]
            source[pl.ds(count * N, count)] = from_below(below)
            source[pl.ds(count * (N + 1), count)] = from_above(above)
            out[...] = product(schwarz[p], source[...])
            first = out[pl.ds(0, count, stride=N)]
            final = out[pl.ds(N - 1, count, stride=N)]
            out[pl.ds(0, count, stride=N)] = first + from_below(final)
            out[pl.ds(N - 1, count, stride=N)] = final + from_above(first)
            out[pl.ds(1, count, stride=N)] += from_below(out[pl.ds(count * (N + 1), count)])
            out[pl.ds(N - 2, count, stride=N)] += from_above(out[pl.ds(count * N, count)])

        for i in range(h):
            if i == 2:
                start(group, LONGEST_FIRST[:6])
            for j in range(h):
                at = pl.ds((i * h + j) * N, N)
                ee, eo, oe, oo = oblk[0, at], oblk[1, at], oblk[2, at], oblk[3, at]
                one, two = pl.ds(j * N, N), pl.ds((N + 1 - j) * N, N)
                loc[i, one] = (ee + eo) + (oe + oo)
                loc[N + 1 - i, one] = (ee + eo) - (oe + oo)
                loc[i, two] = (ee - eo) + (oe - oo)
                loc[N + 1 - i, two] = (ee - eo) - (oe - oo)
        start(group, LONGEST_FIRST[6:])

    def spread_copies(phase, slot, loc):
        return copies(
            phase,
            lambda dx, dy: loc.at[
                span(*part(dx, (0, 2), (N, 2), (1, N))), span(*part(dy, (0, 2), (N, 2), (1, N)), N)
            ],
            lambda m: incoming(sides, corners, slot, m),
        )

    def node_area(field, dx, dy):
        return field.at[span(*part(dx, (N - 2, 2), (0, 2), (0, N))), span(*part(dy, (N - 2, 2), (0, 2), (0, N)), N)]

    porosity = None

    def apply(field, image, group=None):
        for a in range(N // 2):
            lower, upper = field[a], field[N - 1 - a]
            ab[0, pl.ds(a * N * N, N * N)] = lower + upper
            ab[1, pl.ds(a * N * N, N * N)] = lower - upper
        even = product(stiff[0], ab[0])
        odd = product(stiff[1], ab[1])
        for i in range(N // 2):
            at = slice(i * N * N, (i + 1) * N * N)
            scaled = mass[...] * F32(node_weights[i])
            image[i] = porosity * (even[at] + odd[at]) + scaled * field[i]
            image[N - 1 - i] = porosity * (even[at] - odd[at]) + scaled * field[N - 1 - i]
            for a in (i, N - 1 - i):
                first = image[a, pl.ds(0, N, stride=N)]
                final = image[a, pl.ds(N - 1, N, stride=N)]
                image[a, pl.ds(0, N, stride=N)] = first + from_below(final)
                image[a, pl.ds(N - 1, N, stride=N)] = final + from_above(first)
            if i == 1 and group is not None:
                start(group, LONGEST_FIRST[:6])
        if group is not None:
            start(group, LONGEST_FIRST[6:])

    start(halo0)
    loads[0].wait()
    loads[2].wait()
    first_message = total(weighted(lambda a: ext0[a + 1, own])) * send_table[pl.ds(4, 1)]
    gather_y(0, first_message)
    for p in range(4):
        blk[p, pl.ds(248, 8)] = jnp.zeros((8, 128), F32)
    for i, load in enumerate(loads):
        if i not in (0, 2):
            load.wait()
    porosity = 1.0 - 0.6 * grains[...].astype(F32) / MOST_GRAINS
    gather_x(0)
    arrive(halo0)
    spread0 = spread_copies(1, 0, loc0)
    solve(ext0, loc0, spread0)
    gathered(0)
    lifted(0)
    for a in range(N):
        d[a] = loc0[a + 1, own] + lift[0 if a == 0 else (2 if a == N - 1 else 1)]
    arrive(spread0)
    for m, (dx, dy) in enumerate(MOVES):
        area = node_area(d, dx, dy)
        area[...] += incoming(sides, corners, 0, m)[...]

    faces = copies(
        2,
        lambda dx, dy: q1.at[
            span(*part(dx, (0, 2), (N - 2, 2), (0, N))), span(*part(dy, (0, 2), (N - 2, 2), (0, N)), N)
        ],
        lambda m: incoming(sides, corners, 1, m),
    )
    apply(d, q1, faces)
    rho1 = weighted(lambda a: ext0[a + 1, own] * d[a])
    curve = d[0] * q1[0]
    for a in range(1, N):
        curve = curve + d[a] * q1[a]
    gather_y(1, message(classes(lambda a: q1[a], weight_z, (1.0, 1.0, 1.0)), rho1, weight_z * curve))
    for i in (0, N + 1):
        ext1[i] = jnp.zeros_like(ext1[i])
    for a in range(N):
        ext1[a + 1, pl.ds(0, N)] = jnp.zeros((N, 128), F32)
        ext1[a + 1, own] = q1[a]
        ext1[a + 1, pl.ds(N * N + N, N)] = jnp.zeros((N, 128), F32)
    gather_x(1)
    arrive(faces)
    for m, (dx, dy) in enumerate(MOVES):
        area = ext1.at[span(*part(dx, (N, 2), (0, 2), (1, N))), span(*part(dy, (N, 2), (0, 2), (1, N)), N)]
        area[...] += incoming(sides, corners, 1, m)[...]

    spread1 = spread_copies(3, 2, loc1)
    solve(ext1, loc1, spread1)
    gathered(1)
    lifted(1)
    rho1, curve1 = sv[1, pl.ds(9, 1)], sv[1, pl.ds(10, 1)]
    step1 = rho1 / curve1
    for a in range(N):
        z2[a] = d[a] - step1 * (loc1[a + 1, own] + lift[0 if a == 0 else (2 if a == N - 1 else 1)])
        r1[a] = ext0[a + 1, own] - step1 * ext1[a + 1, own]
        sol[a] = sol[a] + step1 * d[a]
    arrive(spread1)
    for m, (dx, dy) in enumerate(MOVES):
        area = node_area(z2, dx, dy)
        area[...] -= step1 * incoming(sides, corners, 2, m)[...]

    apply(z2, q2)
    curve_new = z2[0] * q2[0]
    curve_mixed = z2[0] * q1[0]
    for a in range(1, N):
        curve_new = curve_new + z2[a] * q2[a]
        curve_mixed = curve_mixed + z2[a] * q1[a]
    rho2 = weighted(lambda a: r1[a] * z2[a])
    gather_y(2, message([], rho2, weight_z * curve_new, weight_z * curve_mixed))
    edges = copies(
        4,
        lambda dx, dy: q2.at[
            span(*part(dx, (0, 1), (N - 1, 1), (0, N))), span(*part(dy, (0, 1), (N - 1, 1), (0, N)), N)
        ],
        lambda m: incoming(sides1, corners1, None, m),
    )
    start(edges)
    for a in range(N):
        im2[a] = q2[a]
    gather_x(2)
    arrive(edges)
    for m, (dx, dy) in enumerate(MOVES):
        area = im2.at[
            span(*part(dx, (N - 1, 1), (0, 1), (0, N))), span(*part(dy, (N - 1, 1), (0, 1), (0, N)), N)
        ]
        area[...] += incoming(sides1, corners1, None, m)[...]
    for group in (halo0, spread0, faces, spread1, edges):
        sent(group)
    gathered(2)
    rho2, curve_new, curve_mixed = sv[2, pl.ds(9, 1)], sv[2, pl.ds(10, 1)], sv[2, pl.ds(11, 1)]
    ratio = rho2 / rho1
    step2 = rho2 / (curve_new + ratio * (2.0 * curve_mixed + ratio * curve1))
    for a in range(N):
        direction = z2[a] + ratio * d[a]
        dir_out[0, 0, a] = direction
        sol_out[0, 0, a] = sol[a] + step2 * direction
        res_out[0, 0, a] = r1[a] - step2 * (im2[a] + ratio * ext1[a + 1, own])
    steps_out[0] = step1[0, 0]
    steps_out[1] = step2[0, 0]


def deliver(sol, res, direction, steps, sol_out, res_out, dir_out, steps_out, sems):
    copies = [
        pltpu.make_async_copy(src, dst, sems.at[i])
        for i, (src, dst) in enumerate(
            ((steps, steps_out), (sol, sol_out), (res, res_out), (direction, dir_out))
        )
    ]
    for copy in copies:
        copy.start()
    for copy in copies:
        copy.wait()


def incoming(sides, corners, slot, m):
    first, second = MOVES[m]
    if first and second:
        return corners.at[m - 4] if slot is None else corners.at[slot, m - 4]
    which = 0 if first else 1
    ref = sides[which]
    return ref.at[m % 2] if slot is None else ref.at[slot, m % 2]


def solution(mesh):
    nx, ny = mesh.shape["gx"], mesh.shape["gy"]
    weights, _ = gll_tables()
    send, along_x, back = coarse_tables(nx, ny, 128)
    schwarz, stiff, mass = schwarz_blocks(), stiffness_blocks(), mass_table()
    nn = N * N
    field = pltpu.VMEM((N, nn, 128), F32)
    wide = pltpu.VMEM((N + 2, nn + 2 * N, 128), F32)
    vmem, anywhere = pl.BlockSpec(memory_space=pltpu.VMEM), pl.BlockSpec(memory_space=pl.ANY)
    smem = pl.BlockSpec(memory_space=pltpu.SMEM)

    def step(sol, res, grains):
        shape = sol.shape
        flat = (1, 1, N, nn, 128)
        out = jax.ShapeDtypeStruct(flat, F32)
        outs = pl.pallas_call(
            functools.partial(kernel, nx, ny, [float(v) for v in weights]),
            out_shape=(out, out, out, jax.ShapeDtypeStruct((2,), F32)),
            in_specs=[anywhere] * 9,
            out_specs=(vmem, vmem, vmem, smem),
            scratch_shapes=[
                field, wide, wide,
                pltpu.VMEM((1, 128), jnp.int32),
                pltpu.VMEM((4, 512, 256), BF16),
                pltpu.VMEM((2, 512, 256), BF16),
                pltpu.VMEM((16, 128), F32),
                pltpu.VMEM((3, nx, 128), F32),
                pltpu.VMEM((16, 128), F32),
                pltpu.VMEM((nn, 128), F32),
                pltpu.VMEM((4, 256, 128), F32),
                pltpu.VMEM((4, 256, 128), F32),
                pltpu.VMEM((2, 256, 128), F32),
                wide, wide, field, field, field, field, field, field,
                pltpu.VMEM((3, nn, 128), F32),
                pltpu.VMEM((3, ny, 1, 128), F32),
                pltpu.VMEM((3, nx, 1, 128), F32),
                pltpu.VMEM((3, 16, 128), F32),
                [pltpu.VMEM((3, 2, 2, nn, 128), F32), pltpu.VMEM((3, 2, N, 2 * N, 128), F32)],
                pltpu.VMEM((3, 4, 2, 2 * N, 128), F32),
                [pltpu.VMEM((2, 1, nn, 128), F32), pltpu.VMEM((2, N, N, 128), F32)],
                pltpu.VMEM((4, 1, N, 128), F32),
                pltpu.SemaphoreType.DMA((9,)),
                pltpu.SemaphoreType.DMA((5, 8)),
                pltpu.SemaphoreType.DMA((5, 8)),
                pltpu.SemaphoreType.DMA((3,)),
                pltpu.SemaphoreType.DMA((3,)),
                pltpu.SemaphoreType.DMA((3,)),
                pltpu.SemaphoreType.DMA((3,)),
            ],
            compiler_params=pltpu.CompilerParams(collective_id=0, has_side_effects=True, vmem_limit_bytes=40 * 1024 * 1024),
            name="cg_steps",
        )(
            *(pltpu.with_memory_space_constraint(v, pltpu.HBM) for v in (
            sol.reshape(flat), res.reshape(flat), grains,
            jnp.asarray(schwarz), jnp.asarray(stiff), jnp.asarray(send), jnp.asarray(along_x),
            jnp.asarray(back), jnp.asarray(mass),))
        )
        hbm = pl.BlockSpec(memory_space=pltpu.HBM)
        outs = pl.pallas_call(
            deliver,
            out_shape=(out, out, out, jax.ShapeDtypeStruct((2,), F32)),
            in_specs=[anywhere] * 4,
            out_specs=(hbm,) * 4,
            scratch_shapes=[pltpu.SemaphoreType.DMA((4,))],
            compiler_params=pltpu.CompilerParams(vmem_limit_bytes=2 * 1024 * 1024),
            name="deliver",
        )(*outs)
        return tuple(v.reshape(shape) for v in outs[:3]) + (outs[3],)

    wide_spec = P("gx", "gy", None, None, None, None)
    return jax.shard_map(
        step,
        mesh=mesh,
        in_specs=(wide_spec, wide_spec, P("gx", "gy", None)),
        out_specs=(wide_spec, wide_spec, wide_spec, P()),
        check_vma=False,
    )
```

```python
import functools
import math

import jax
import jax.numpy as jnp
import ml_dtypes
import numpy as np
from jax import lax
from jax.experimental import pallas as pl
from jax.experimental.pallas import tpu as pltpu
from jax.sharding import PartitionSpec as P

N = 8
MOST_GRAINS = 16
shift_mass = 0.1
mean_porosity = 0.7
MESH = pl.DeviceIdType.MESH
F32 = jnp.float32
BF16 = jnp.bfloat16
MOVES = [(1, 0), (-1, 0), (0, 1), (0, -1), (1, 1), (1, -1), (-1, 1), (-1, -1)]
LONGEST_FIRST = [4, 5, 6, 7, 0, 1, 2, 3]
NEAREST_FIRST = [2, 3, 0, 1, 4, 5, 6, 7]
PLAIN = 48


def legendre_columns(node_set, degree):
    table = [node_set * 0.0 + 1.0, node_set]
    for order in range(2, degree + 1):
        table.append(((2 * order - 1) * node_set * table[order - 1] - (order - 1) * table[order - 2]) / order)
    return table


def gll_tables():
    degree = N - 1
    node_set = np.cos(math.pi * np.arange(degree + 1) / degree)
    for _ in range(100):
        table = legendre_columns(node_set, degree)
        node_set = node_set - (node_set * table[degree] - table[degree - 1]) / ((degree + 1) * table[degree])
    node_set = node_set[::-1].copy()
    values = legendre_columns(node_set, degree)[degree]
    weights = 2.0 / (degree * (degree + 1) * values**2)
    derivative = np.zeros((N, N))
    for a in range(N):
        for b in range(N):
            if a != b:
                derivative[a, b] = values[a] / (values[b] * (node_set[a] - node_set[b]))
    derivative[0, 0] = -degree * (degree + 1) / 4.0
    derivative[N - 1, N - 1] = degree * (degree + 1) / 4.0
    return weights, derivative


def schwarz_tables():
    weights, derivative = gll_tables()
    stiffness = derivative.T @ (weights[:, None] * derivative)
    total = 3 * (N - 1) + 1
    three_stiffness = np.zeros((total, total))
    three_mass = np.zeros(total)
    for element in range(3):
        at = element * (N - 1)
        three_stiffness[at : at + N, at : at + N] += stiffness
        three_mass[at : at + N] += weights
    chosen = np.array([N - 2] + list(range(N - 1, 2 * N - 1)) + [2 * N - 1])
    scaling = 1.0 / np.sqrt(three_mass[chosen])
    symmetric = scaling[:, None] * three_stiffness[chosen][:, chosen] * scaling[None, :]
    values, vectors = np.linalg.eigh(0.5 * (symmetric + symmetric.T))
    return scaling[:, None] * vectors, values


def hi_lo(matrix):
    high = matrix.astype(ml_dtypes.bfloat16)
    low = (matrix - high.astype(np.float64)).astype(ml_dtypes.bfloat16)
    return np.concatenate([high, low], axis=-1)


def schwarz_blocks():
    basis, values = schwarz_tables()
    m = N + 2
    divisor = mean_porosity * (values[:, None, None] + values[None, :, None] + values[None, None, :]) + shift_mass
    fold = np.zeros((2, m // 2, m))
    for i in range(m // 2):
        fold[0, i, i] = fold[0, i, m - 1 - i] = 1.0
        fold[1, i, i], fold[1, i, m - 1 - i] = 1.0, -1.0
    order = np.zeros((m // 2, m // 2, m), np.int64)
    for i in range(m // 2):
        for j in range(m // 2):
            at = i * (m // 2) + j
            order[i, j, 1 : m - 1] = at * N + np.arange(N)
            order[i, j, 0] = (m // 2) ** 2 * N + at
            order[i, j, m - 1] = (m // 2) ** 2 * (N + 1) + at
    order = order.reshape(-1)
    blocks = np.zeros((4, 256, 256))
    for p in range(2):
        for q in range(2):
            left = np.kron(np.kron(fold[p] @ basis, fold[q] @ basis), basis)
            block = (left / divisor.reshape(-1)) @ left.T / 16.0
            blocks[2 * p + q][np.ix_(order, order)] = block
    return hi_lo(blocks)


def stiffness_blocks():
    weights, derivative = gll_tables()
    one = derivative.T @ (weights[:, None] * derivative)
    mass = np.diag(weights)
    whole = (
        np.kron(np.kron(one, mass), mass) + np.kron(np.kron(mass, one), mass) + np.kron(np.kron(mass, mass), one)
    )
    half = N // 2 * N * N
    blocks = np.zeros((2, half, half))
    for p, sign in enumerate((1.0, -1.0)):
        fold = np.zeros((N // 2, N))
        for i in range(N // 2):
            fold[i, i], fold[i, N - 1 - i] = 1.0, sign
        fold = np.kron(fold, np.eye(N * N))
        blocks[p] = fold @ whole @ fold.T / 4.0
    return hi_lo(blocks)


def cosine_basis(count):
    position = np.arange(count, dtype=np.float64)
    phase = math.pi * (position[:, None] + 0.5) * position[None, :] / count
    norm = np.where(position == 0, math.sqrt(1.0 / count), math.sqrt(2.0 / count))
    return np.cos(phase) * norm[None, :], 2.0 - 2.0 * np.cos(math.pi * position / count)


def share_rows(count):
    table = np.zeros((count, 3, count))
    for at in range(count):
        table[at, :, at] = 1.0
        if at > 0:
            table[at, 0, at], table[at, 0, at - 1] = 0.5, 0.5
        if at < count - 1:
            table[at, 2, at], table[at, 2, at + 1] = 0.5, 0.5
    return table


def coarse_tables(nx, ny, length):
    first, eigen_first = cosine_basis(nx)
    second, eigen_second = cosine_basis(ny)
    divisor = (
        2.0 * mean_porosity * length * (eigen_first[:, None] + eigen_second[None, :]) + 8.0 * shift_mass * length
    )
    share_first, share_second = share_rows(nx), share_rows(ny)
    green = np.einsum("ap,bp,pk->kab", first, first, 1.0 / divisor)
    send = np.zeros((ny, 16, 128))
    back = np.zeros((ny, 16, 128))
    along_x = np.ones((nx, 3, nx, 128))
    for t in range(3):
        lanes = slice(t * ny, (t + 1) * ny)
        for s in range(3):
            modes = share_second[:, s] @ second
            send[:, 3 * t + s, lanes] = modes
            for other in range(3):
                back[:, 3 * other + s, lanes] = modes
        for other in range(3):
            along_x[:, other, :, lanes] = np.einsum("xc,kcd,bd->xbk", share_first[:, other], green, share_first[:, t])
    for row in range(3):
        send[:, 9 + row, PLAIN + 16 * row] = 1.0
        back[:, 9 + row, PLAIN + 16 * row] = 1.0
    return send.astype(np.float32), along_x.astype(np.float32), back.astype(np.float32)


def mass_table():
    weights, _ = gll_tables()
    table = shift_mass * (weights[:, None] * weights[None, :]).reshape(N * N, 1)
    return np.broadcast_to(table, (N * N, 128)).astype(np.float32).copy()


def part(step, low, high, whole):
    return low if step < 0 else (high if step > 0 else whole)


def span(first, count, unit=1):
    return pl.ds(first * unit, count * unit)


def kernel(
    nx, ny, node_weights,
    sol_in, res_in, grains_in, schwarz_in, stiff_in, send_in, along_x_in, back_in, mass_in,
    sol_out, res_out, dir_out, steps_out,
    sol, ext0, ext1, grains, schwarz, stiff, send_table, along_x, back, mass,
    blk, oblk, ab, loc0, loc1, d, q1, z2, q2, r1, im2, lift, buf_y, buf_x, sv, sides, corners, sides1, corners1,
    load_sem, send_sem, recv_sem, gy_send, gy_recv, gx_send, gx_recv,
):
    x, y = lax.axis_index("gx"), lax.axis_index("gy")

    def inside(dx, dy):
        checks = []
        if dx > 0:
            checks.append(x < nx - 1)
        if dx < 0:
            checks.append(x > 0)
        if dy > 0:
            checks.append(y < ny - 1)
        if dy < 0:
            checks.append(y > 0)
        return functools.reduce(jnp.logical_and, checks)

    barrier = pltpu.get_barrier_semaphore()

    expected = jnp.int32(nx - 1 + ny - 1)
    for dx, dy in MOVES:
        there = inside(dx, dy)
        if dx and dy:
            expected = expected + there.astype(jnp.int32)

        @pl.when(there)
        def _():
            pl.semaphore_signal(barrier, inc=1, device_id=(x + dx, y + dy), device_id_type=MESH)

    @pl.loop(0, nx)
    def _(k):
        @pl.when((k > x + 1) | (k < x - 1))
        def _():
            pl.semaphore_signal(barrier, inc=1, device_id=(k, y), device_id_type=MESH)

    @pl.loop(0, ny)
    def _(k):
        @pl.when((k > y + 1) | (k < y - 1))
        def _():
            pl.semaphore_signal(barrier, inc=1, device_id=(x, k), device_id_type=MESH)

    loads = [
        pltpu.make_async_copy(src, dst, load_sem.at[i])
        for i, (src, dst) in enumerate(
            [
                (res_in.at[0, 0], ext0.at[pl.ds(1, N), pl.ds(N, N * N)]),
                (schwarz_in, schwarz.at[:, :, pl.ds(0, 512)]),
                (send_in.at[y], send_table),
                (along_x_in.at[x], along_x),
                (back_in.at[y], back),
                (grains_in.at[0], grains),
                (stiff_in, stiff.at[:, :, pl.ds(0, 512)]),
                (schwarz_in.at[:, :, pl.ds(0, 256)], schwarz.at[:, :, pl.ds(512, 256)]),
                (stiff_in.at[:, :, pl.ds(0, 256)], stiff.at[:, :, pl.ds(512, 256)]),
                (mass_in, mass),
                (sol_in.at[0, 0], sol),
            ]
        )
    ]
    for load in loads:
        load.start()

    for m, (dx, dy) in enumerate(MOVES):

        @pl.when(jnp.logical_not(inside(-dx, -dy)))
        def _():
            area = ext0.at[span(*part(dx, (N + 1, 1), (0, 1), (1, N))), span(*part(dy, (N + 1, 1), (0, 1), (1, N)), N)]
            area[...] = jnp.zeros_like(area)

    lane = lax.broadcasted_iota(jnp.int32, (1, 128), 1)
    last = 127
    row = lax.broadcasted_iota(jnp.int32, (N * N, 128), 0)
    wide = lax.broadcasted_iota(jnp.int32, (N * N, 128), 1)
    inner = lax.rem(row, N)
    shared_z = ((inner == 0) & (wide > 0)) | ((inner == N - 1) & (wide < last))
    weight_z = jnp.where(shared_z, 0.5, 1.0).astype(F32)
    low_y = jnp.where(y > 0, 0.5, 1.0).astype(F32)
    high_y = jnp.where(y < ny - 1, 0.5, 1.0).astype(F32)
    low_x = jnp.where(x > 0, 0.5, 1.0).astype(F32)
    high_x = jnp.where(x < nx - 1, 0.5, 1.0).astype(F32)
    weight_yz = weight_z * jnp.where(row < N, low_y, jnp.where(row >= N * N - N, high_y, 1.0))

    def from_below(v):
        return jnp.where(lane > 0, pltpu.roll(v, 1, axis=1), 0.0)

    def from_above(v):
        return jnp.where(lane < last, pltpu.roll(v, last, axis=1), 0.0)

    def total(v):
        return jnp.sum(jnp.sum(v, axis=0, keepdims=True), axis=1, keepdims=True)

    def weighted(product):
        middle = product(1)
        for a in range(2, N - 1):
            middle = middle + product(a)
        return weight_yz * (low_x * product(0) + middle + high_x * product(N - 1))

    own = pl.ds(N, N * N)

    def classes(field, weight, ends):
        middle = field(1)
        for a in range(2, N - 1):
            middle = middle + field(a)
        rows = []
        for scale, value in zip(ends, (field(0), middle, field(N - 1))):
            value = value * weight * scale
            inner_rows = value[N : 2 * N]
            for b in range(2, N - 1):
                inner_rows = inner_rows + value[b * N : b * N + N]
            for part_rows in (value[:N], inner_rows, value[N * N - N :]):
                rows.append(jnp.sum(part_rows, axis=0, keepdims=True))
        return rows

    def message(rows, *sums):
        result = jnp.zeros((1, 128), F32)
        for i, value in enumerate(rows):
            result = result + jnp.sum(value, axis=1, keepdims=True) * send_table[pl.ds(i, 1)]
        for i, value in enumerate(sums):
            result = result + total(value) * send_table[pl.ds(9 + i, 1)]
        return result

    loads[0].wait()
    loads[2].wait()
    first_message = total(weighted(lambda a: ext0[a + 1, own])) * send_table[pl.ds(4, 1)]
    pl.semaphore_wait(barrier, expected)

    def copies(phase, source, target):
        return [
            pltpu.make_async_remote_copy(
                src_ref=source(dx, dy),
                dst_ref=target(m),
                send_sem=send_sem.at[phase, m],
                recv_sem=recv_sem.at[phase, m],
                device_id=(x + dx, y + dy),
                device_id_type=MESH,
            )
            for m, (dx, dy) in enumerate(MOVES)
        ]

    def start(group, moves=LONGEST_FIRST):
        for m in moves:
            pl.when(inside(*MOVES[m]))(group[m].start)

    def arrive(group):
        for m, (dx, dy) in enumerate(MOVES):
            pl.when(inside(-dx, -dy))(group[m].wait_recv)

    def arrive_and_add(group, area, slot, scale=None):
        for m in NEAREST_FIRST:
            dx, dy = MOVES[m]

            @pl.when(inside(-dx, -dy))
            def _():
                group[m].wait_recv()
                target = area(dx, dy)
                value = incoming(*slot, m)[...]
                target[...] += value if scale is None else scale * value

    def sent(group):
        for m, (dx, dy) in enumerate(MOVES):
            pl.when(inside(dx, dy))(group[m].wait_send)

    def ext_target(m):
        dx, dy = MOVES[m]
        return ext0.at[span(*part(dx, (N + 1, 1), (0, 1), (1, N))), span(*part(dy, (N + 1, 1), (0, 1), (1, N)), N)]

    halo0 = copies(
        0,
        lambda dx, dy: res_in.at[
            0, 0, span(*part(dx, (1, 1), (N - 2, 1), (0, N))), span(*part(dy, (1, 1), (N - 2, 1), (0, N)), N)
        ],
        ext_target,
    )

    def stage(buffer, index, send, recv, count, device):
        def copy(k):
            return pltpu.make_async_remote_copy(
                src_ref=buffer.at[pl.ds(index, 1)],
                dst_ref=buffer.at[pl.ds(index, 1)],
                send_sem=send,
                recv_sem=recv,
                device_id=device(k),
                device_id_type=MESH,
            )

        @pl.loop(1, count)
        def _(k):
            copy(k).start()

    def all_rows(buffer, send, recv, count):
        rows = buffer.at[pl.ds(0, count - 1)]
        pltpu.make_async_copy(rows, rows, recv).wait()
        pltpu.make_async_copy(rows, rows, send).wait()

    def gather_y(g, value):
        buf_y[g, pl.ds(y, 1)] = value.reshape(1, 1, 128)
        stage(buf_y.at[g], y, gy_send.at[g], gy_recv.at[g], ny, lambda k: (x, lax.rem(y + k, ny)))

    def gather_x(g):
        all_rows(buf_y.at[g], gy_send.at[g], gy_recv.at[g], ny)
        value = jnp.sum(buf_y[g], axis=0)
        buf_x[g, pl.ds(x, 1)] = value.reshape(1, 1, 128)
        stage(buf_x.at[g], x, gx_send.at[g], gx_recv.at[g], nx, lambda k: (lax.rem(x + k, nx), y))

    def gathered(g):
        all_rows(buf_x.at[g], gx_send.at[g], gx_recv.at[g], nx)
        rows = buf_x[g].reshape(nx, 128)
        low, middle, high = (jnp.sum(rows * along_x[t], axis=0, keepdims=True) for t in range(3))
        row16 = lax.broadcasted_iota(jnp.int32, (16, 128), 0)
        value = jnp.where(row16 < 3, low, jnp.where(row16 < 6, middle, high))
        sums = jnp.sum(value * back[...], axis=1, keepdims=True)
        sv[g] = jnp.broadcast_to(sums, (16, 128))

    def lifted(g):
        for t in range(3):
            for s in range(3):
                at, count = ((0, 1), (1, N - 2), (N - 1, 1))[s]
                lift[t, pl.ds(at * N, count * N)] = jnp.broadcast_to(sv[g, pl.ds(3 * t + s, 1)], (count * N, 128))

    def product(matrix, v):
        high = v.astype(BF16)
        low = (v - high.astype(F32)).astype(BF16)
        return jnp.dot(matrix, jnp.concatenate([high, high, low], axis=0), preferred_element_type=F32)

    def solve(ext, loc, group):
        h = (N + 2) // 2
        for i in range(h):
            lower, upper = ext[i], ext[N + 1 - i]
            even, odd = lower + upper, lower - upper
            for j in range(h):
                one, two = slice(j * N, j * N + N), slice((N + 1 - j) * N, (N + 2 - j) * N)
                at = pl.ds((i * h + j) * N, N)
                blk[0, at] = even[one] + even[two]
                blk[1, at] = even[one] - even[two]
                blk[2, at] = odd[one] + odd[two]
                blk[3, at] = odd[one] - odd[two]
        count = h * h

        for p in range(4):
            source = blk.at[p]
            below = source[pl.ds(N - 2, count, stride=N)]
            above = source[pl.ds(1, count, stride=N)]
            source[pl.ds(count * N, count)] = from_below(below)
            source[pl.ds(count * (N + 1), count)] = from_above(above)
        for p in range(4):
            out = oblk.at[p]
            out[...] = product(schwarz[p], blk[p])
            first = out[pl.ds(0, count, stride=N)]
            final = out[pl.ds(N - 1, count, stride=N)]
            out[pl.ds(0, count, stride=N)] = first + from_below(final)
            out[pl.ds(N - 1, count, stride=N)] = final + from_above(first)
            out[pl.ds(1, count, stride=N)] += from_below(out[pl.ds(count * (N + 1), count)])
            out[pl.ds(N - 2, count, stride=N)] += from_above(out[pl.ds(count * N, count)])

        for i in range(h):
            if i == 2:
                start(group, LONGEST_FIRST[:6])
            for j in range(h):
                at = pl.ds((i * h + j) * N, N)
                ee, eo, oe, oo = oblk[0, at], oblk[1, at], oblk[2, at], oblk[3, at]
                one, two = pl.ds(j * N, N), pl.ds((N + 1 - j) * N, N)
                loc[i, one] = (ee + eo) + (oe + oo)
                loc[N + 1 - i, one] = (ee + eo) - (oe + oo)
                loc[i, two] = (ee - eo) + (oe - oo)
                loc[N + 1 - i, two] = (ee - eo) - (oe - oo)
        start(group, LONGEST_FIRST[6:])

    def spread_copies(phase, slot, loc):
        return copies(
            phase,
            lambda dx, dy: loc.at[
                span(*part(dx, (0, 2), (N, 2), (1, N))), span(*part(dy, (0, 2), (N, 2), (1, N)), N)
            ],
            lambda m: incoming(sides, corners, slot, m),
        )

    def node_area(field, dx, dy):
        return field.at[span(*part(dx, (N - 2, 2), (0, 2), (0, N))), span(*part(dy, (N - 2, 2), (0, 2), (0, N)), N)]

    porosity = None

    def apply(field, image, group=None):
        for a in range(N // 2):
            lower, upper = field[a], field[N - 1 - a]
            ab[0, pl.ds(a * N * N, N * N)] = lower + upper
            ab[1, pl.ds(a * N * N, N * N)] = lower - upper
        even = product(stiff[0], ab[0])
        odd = product(stiff[1], ab[1])
        for i in range(N // 2):
            at = slice(i * N * N, (i + 1) * N * N)
            scaled = mass[...] * F32(node_weights[i])
            image[i] = porosity * (even[at] + odd[at]) + scaled * field[i]
            image[N - 1 - i] = porosity * (even[at] - odd[at]) + scaled * field[N - 1 - i]
            for a in (i, N - 1 - i):
                first = image[a, pl.ds(0, N, stride=N)]
                final = image[a, pl.ds(N - 1, N, stride=N)]
                image[a, pl.ds(0, N, stride=N)] = first + from_below(final)
                image[a, pl.ds(N - 1, N, stride=N)] = final + from_above(first)
            if i == 1 and group is not None:
                start(group, LONGEST_FIRST[:6])
        if group is not None:
            start(group, LONGEST_FIRST[6:])

    gather_y(0, first_message)
    start(halo0)
    for p in range(4):
        blk[p, pl.ds(248, 8)] = jnp.zeros((8, 128), F32)
    for i, load in enumerate(loads):
        if i not in (0, 2):
            load.wait()
    porosity = 1.0 - 0.6 * grains[...].astype(F32) / MOST_GRAINS
    gather_x(0)
    arrive(halo0)
    spread0 = spread_copies(1, 0, loc0)
    solve(ext0, loc0, spread0)
    gathered(0)
    lifted(0)
    for a in range(N):
        d[a] = loc0[a + 1, own] + lift[0 if a == 0 else (2 if a == N - 1 else 1)]
    arrive_and_add(spread0, lambda dx, dy: node_area(d, dx, dy), (sides, corners, 0))

    faces = copies(
        2,
        lambda dx, dy: q1.at[
            span(*part(dx, (0, 2), (N - 2, 2), (0, N))), span(*part(dy, (0, 2), (N - 2, 2), (0, N)), N)
        ],
        lambda m: incoming(sides, corners, 1, m),
    )
    apply(d, q1, faces)
    rho1 = weighted(lambda a: ext0[a + 1, own] * d[a])
    curve = d[0] * q1[0]
    for a in range(1, N):
        curve = curve + d[a] * q1[a]
    gather_y(1, message(classes(lambda a: q1[a], weight_z, (1.0, 1.0, 1.0)), rho1, weight_z * curve))
    for i in (0, N + 1):
        ext1[i] = jnp.zeros_like(ext1[i])
    for a in range(N):
        ext1[a + 1, pl.ds(0, N)] = jnp.zeros((N, 128), F32)
        ext1[a + 1, own] = q1[a]
        ext1[a + 1, pl.ds(N * N + N, N)] = jnp.zeros((N, 128), F32)
    gather_x(1)
    arrive_and_add(
        faces,
        lambda dx, dy: ext1.at[span(*part(dx, (N, 2), (0, 2), (1, N))), span(*part(dy, (N, 2), (0, 2), (1, N)), N)],
        (sides, corners, 1),
    )

    spread1 = spread_copies(3, 2, loc1)
    solve(ext1, loc1, spread1)
    gathered(1)
    lifted(1)
    rho1, curve1 = sv[1, pl.ds(9, 1)], sv[1, pl.ds(10, 1)]
    step1 = rho1 / curve1
    for a in range(N):
        z2[a] = d[a] - step1 * (loc1[a + 1, own] + lift[0 if a == 0 else (2 if a == N - 1 else 1)])
        r1[a] = ext0[a + 1, own] - step1 * ext1[a + 1, own]
        sol[a] = sol[a] + step1 * d[a]
    arrive_and_add(spread1, lambda dx, dy: node_area(z2, dx, dy), (sides, corners, 2), -step1)

    apply(z2, q2)
    curve_new = z2[0] * q2[0]
    curve_mixed = z2[0] * q1[0]
    for a in range(1, N):
        curve_new = curve_new + z2[a] * q2[a]
        curve_mixed = curve_mixed + z2[a] * q1[a]
    rho2 = weighted(lambda a: r1[a] * z2[a])
    gather_y(2, message([], rho2, weight_z * curve_new, weight_z * curve_mixed))
    edges = copies(
        4,
        lambda dx, dy: q2.at[
            span(*part(dx, (0, 1), (N - 1, 1), (0, N))), span(*part(dy, (0, 1), (N - 1, 1), (0, N)), N)
        ],
        lambda m: incoming(sides1, corners1, None, m),
    )
    start(edges)
    for a in range(N):
        im2[a] = q2[a]
    gather_x(2)
    arrive_and_add(
        edges,
        lambda dx, dy: im2.at[
            span(*part(dx, (N - 1, 1), (0, 1), (0, N))), span(*part(dy, (N - 1, 1), (0, 1), (0, N)), N)
        ],
        (sides1, corners1, None),
    )
    for group in (halo0, spread0, faces, spread1, edges):
        sent(group)
    all_rows(buf_x.at[2], gx_send.at[2], gx_recv.at[2], nx)
    value = jnp.sum(buf_x[2], axis=0)
    rho2, curve_new, curve_mixed = (
        jnp.sum(jnp.where(lane == PLAIN + 16 * i, value, 0.0), axis=1, keepdims=True) for i in range(3)
    )
    ratio = rho2 / rho1
    step2 = rho2 / (curve_new + ratio * (2.0 * curve_mixed + ratio * curve1))
    for a in range(N):
        direction = z2[a] + ratio * d[a]
        dir_out[0, 0, a] = direction
        sol_out[0, 0, a] = sol[a] + step2 * direction
        res_out[0, 0, a] = r1[a] - step2 * (im2[a] + ratio * ext1[a + 1, own])
    steps_out[0] = step1[0, 0]
    steps_out[1] = step2[0, 0]


def deliver(sol, res, direction, steps, sol_out, res_out, dir_out, steps_out, sems):
    copies = [
        pltpu.make_async_copy(src, dst, sems.at[i])
        for i, (src, dst) in enumerate(
            ((steps, steps_out), (sol, sol_out), (res, res_out), (direction, dir_out))
        )
    ]
    for copy in copies:
        copy.start()
    for copy in copies:
        copy.wait()


def incoming(sides, corners, slot, m):
    first, second = MOVES[m]
    if first and second:
        return corners.at[m - 4] if slot is None else corners.at[slot, m - 4]
    which = 0 if first else 1
    ref = sides[which]
    return ref.at[m % 2] if slot is None else ref.at[slot, m % 2]


def solution(mesh):
    nx, ny = mesh.shape["gx"], mesh.shape["gy"]
    weights, _ = gll_tables()
    send, along_x, back = coarse_tables(nx, ny, 128)
    schwarz, stiff, mass = schwarz_blocks(), stiffness_blocks(), mass_table()
    nn = N * N
    field = pltpu.VMEM((N, nn, 128), F32)
    wide = pltpu.VMEM((N + 2, nn + 2 * N, 128), F32)
    vmem, anywhere = pl.BlockSpec(memory_space=pltpu.VMEM), pl.BlockSpec(memory_space=pl.ANY)
    smem = pl.BlockSpec(memory_space=pltpu.SMEM)

    def step(sol, res, grains):
        shape = sol.shape
        flat = (1, 1, N, nn, 128)
        out = jax.ShapeDtypeStruct(flat, F32)
        outs = pl.pallas_call(
            functools.partial(kernel, nx, ny, [float(v) for v in weights]),
            out_shape=(out, out, out, jax.ShapeDtypeStruct((2,), F32)),
            in_specs=[anywhere] * 9,
            out_specs=(vmem, vmem, vmem, smem),
            scratch_shapes=[
                field, wide, wide,
                pltpu.VMEM((1, 128), jnp.int32),
                pltpu.VMEM((4, 256, 768), BF16),
                pltpu.VMEM((2, 256, 768), BF16),
                pltpu.VMEM((16, 128), F32),
                pltpu.VMEM((3, nx, 128), F32),
                pltpu.VMEM((16, 128), F32),
                pltpu.VMEM((nn, 128), F32),
                pltpu.VMEM((4, 256, 128), F32),
                pltpu.VMEM((4, 256, 128), F32),
                pltpu.VMEM((2, 256, 128), F32),
                wide, wide, field, field, field, field, field, field,
                pltpu.VMEM((3, nn, 128), F32),
                pltpu.VMEM((3, ny, 1, 128), F32),
                pltpu.VMEM((3, nx, 1, 128), F32),
                pltpu.VMEM((3, 16, 128), F32),
                [pltpu.VMEM((3, 2, 2, nn, 128), F32), pltpu.VMEM((3, 2, N, 2 * N, 128), F32)],
                pltpu.VMEM((3, 4, 2, 2 * N, 128), F32),
                [pltpu.VMEM((2, 1, nn, 128), F32), pltpu.VMEM((2, N, N, 128), F32)],
                pltpu.VMEM((4, 1, N, 128), F32),
                pltpu.SemaphoreType.DMA((11,)),
                pltpu.SemaphoreType.DMA((5, 8)),
                pltpu.SemaphoreType.DMA((5, 8)),
                pltpu.SemaphoreType.DMA((3,)),
                pltpu.SemaphoreType.DMA((3,)),
                pltpu.SemaphoreType.DMA((3,)),
                pltpu.SemaphoreType.DMA((3,)),
            ],
            compiler_params=pltpu.CompilerParams(collective_id=0, has_side_effects=True, vmem_limit_bytes=40 * 1024 * 1024),
            name="cg_steps",
        )(
            *(pltpu.with_memory_space_constraint(v, pltpu.HBM) for v in (
            sol.reshape(flat), res.reshape(flat), grains,
            jnp.asarray(schwarz), jnp.asarray(stiff), jnp.asarray(send), jnp.asarray(along_x),
            jnp.asarray(back), jnp.asarray(mass),))
        )
        hbm = pl.BlockSpec(memory_space=pltpu.HBM)
        outs = pl.pallas_call(
            deliver,
            out_shape=(out, out, out, jax.ShapeDtypeStruct((2,), F32)),
            in_specs=[anywhere] * 4,
            out_specs=(hbm,) * 4,
            scratch_shapes=[pltpu.SemaphoreType.DMA((4,))],
            compiler_params=pltpu.CompilerParams(vmem_limit_bytes=2 * 1024 * 1024),
            name="deliver",
        )(*outs)
        return tuple(v.reshape(shape) for v in outs[:3]) + (outs[3],)

    wide_spec = P("gx", "gy", None, None, None, None)
    return jax.shard_map(
        step,
        mesh=mesh,
        in_specs=(wide_spec, wide_spec, P("gx", "gy", None)),
        out_specs=(wide_spec, wide_spec, wide_spec, P()),
        check_vma=False,
    )
```

```python
import functools
import math

import jax
import jax.numpy as jnp
import ml_dtypes
import numpy as np
from jax import lax
from jax.experimental import pallas as pl
from jax.experimental.pallas import tpu as pltpu
from jax.sharding import PartitionSpec as P

N = 8
MOST_GRAINS = 16
shift_mass = 0.1
mean_porosity = 0.7
MESH = pl.DeviceIdType.MESH
F32 = jnp.float32
BF16 = jnp.bfloat16
MOVES = [(1, 0), (-1, 0), (0, 1), (0, -1), (1, 1), (1, -1), (-1, 1), (-1, -1)]
LONGEST_FIRST = [4, 5, 6, 7, 0, 1, 2, 3]
NEAREST_FIRST = [2, 3, 0, 1, 4, 5, 6, 7]
PLAIN = 48


def legendre_columns(node_set, degree):
    table = [node_set * 0.0 + 1.0, node_set]
    for order in range(2, degree + 1):
        table.append(((2 * order - 1) * node_set * table[order - 1] - (order - 1) * table[order - 2]) / order)
    return table


def gll_tables():
    degree = N - 1
    node_set = np.cos(math.pi * np.arange(degree + 1) / degree)
    for _ in range(100):
        table = legendre_columns(node_set, degree)
        node_set = node_set - (node_set * table[degree] - table[degree - 1]) / ((degree + 1) * table[degree])
    node_set = node_set[::-1].copy()
    values = legendre_columns(node_set, degree)[degree]
    weights = 2.0 / (degree * (degree + 1) * values**2)
    derivative = np.zeros((N, N))
    for a in range(N):
        for b in range(N):
            if a != b:
                derivative[a, b] = values[a] / (values[b] * (node_set[a] - node_set[b]))
    derivative[0, 0] = -degree * (degree + 1) / 4.0
    derivative[N - 1, N - 1] = degree * (degree + 1) / 4.0
    return weights, derivative


def schwarz_tables():
    weights, derivative = gll_tables()
    stiffness = derivative.T @ (weights[:, None] * derivative)
    total = 3 * (N - 1) + 1
    three_stiffness = np.zeros((total, total))
    three_mass = np.zeros(total)
    for element in range(3):
        at = element * (N - 1)
        three_stiffness[at : at + N, at : at + N] += stiffness
        three_mass[at : at + N] += weights
    chosen = np.array([N - 2] + list(range(N - 1, 2 * N - 1)) + [2 * N - 1])
    scaling = 1.0 / np.sqrt(three_mass[chosen])
    symmetric = scaling[:, None] * three_stiffness[chosen][:, chosen] * scaling[None, :]
    values, vectors = np.linalg.eigh(0.5 * (symmetric + symmetric.T))
    return scaling[:, None] * vectors, values


def hi_lo(matrix):
    high = matrix.astype(ml_dtypes.bfloat16)
    low = (matrix - high.astype(np.float64)).astype(ml_dtypes.bfloat16)
    return np.concatenate([high, low], axis=-1)


def schwarz_blocks():
    basis, values = schwarz_tables()
    m = N + 2
    divisor = mean_porosity * (values[:, None, None] + values[None, :, None] + values[None, None, :]) + shift_mass
    fold = np.zeros((2, m // 2, m))
    for i in range(m // 2):
        fold[0, i, i] = fold[0, i, m - 1 - i] = 1.0
        fold[1, i, i], fold[1, i, m - 1 - i] = 1.0, -1.0
    order = np.zeros((m // 2, m // 2, m), np.int64)
    for i in range(m // 2):
        for j in range(m // 2):
            at = i * (m // 2) + j
            order[i, j, 1 : m - 1] = at * N + np.arange(N)
            order[i, j, 0] = (m // 2) ** 2 * N + at
            order[i, j, m - 1] = (m // 2) ** 2 * (N + 1) + at
    order = order.reshape(-1)
    blocks = np.zeros((4, 256, 256))
    for p in range(2):
        for q in range(2):
            left = np.kron(np.kron(fold[p] @ basis, fold[q] @ basis), basis)
            block = (left / divisor.reshape(-1)) @ left.T / 16.0
            blocks[2 * p + q][np.ix_(order, order)] = block
    return hi_lo(blocks)


def stiffness_blocks():
    weights, derivative = gll_tables()
    one = derivative.T @ (weights[:, None] * derivative)
    mass = np.diag(weights)
    whole = (
        np.kron(np.kron(one, mass), mass) + np.kron(np.kron(mass, one), mass) + np.kron(np.kron(mass, mass), one)
    )
    half = N // 2 * N * N
    blocks = np.zeros((2, half, half))
    for p, sign in enumerate((1.0, -1.0)):
        fold = np.zeros((N // 2, N))
        for i in range(N // 2):
            fold[i, i], fold[i, N - 1 - i] = 1.0, sign
        fold = np.kron(fold, np.eye(N * N))
        blocks[p] = fold @ whole @ fold.T / 4.0
    return hi_lo(blocks)


def cosine_basis(count):
    position = np.arange(count, dtype=np.float64)
    phase = math.pi * (position[:, None] + 0.5) * position[None, :] / count
    norm = np.where(position == 0, math.sqrt(1.0 / count), math.sqrt(2.0 / count))
    return np.cos(phase) * norm[None, :], 2.0 - 2.0 * np.cos(math.pi * position / count)


def share_rows(count):
    table = np.zeros((count, 3, count))
    for at in range(count):
        table[at, :, at] = 1.0
        if at > 0:
            table[at, 0, at], table[at, 0, at - 1] = 0.5, 0.5
        if at < count - 1:
            table[at, 2, at], table[at, 2, at + 1] = 0.5, 0.5
    return table


def coarse_tables(nx, ny, length):
    first, eigen_first = cosine_basis(nx)
    second, eigen_second = cosine_basis(ny)
    divisor = (
        2.0 * mean_porosity * length * (eigen_first[:, None] + eigen_second[None, :]) + 8.0 * shift_mass * length
    )
    share_first, share_second = share_rows(nx), share_rows(ny)
    green = np.einsum("ap,bp,pk->kab", first, first, 1.0 / divisor)
    send = np.zeros((ny, 16, 128))
    back = np.zeros((ny, 16, 128))
    along_x = np.ones((nx, 3, nx, 128))
    for t in range(3):
        lanes = slice(t * ny, (t + 1) * ny)
        for s in range(3):
            modes = share_second[:, s] @ second
            send[:, 3 * t + s, lanes] = modes
            for other in range(3):
                back[:, 3 * other + s, lanes] = modes
        for other in range(3):
            along_x[:, other, :, lanes] = np.einsum("xc,kcd,bd->xbk", share_first[:, other], green, share_first[:, t])
    for row in range(3):
        send[:, 9 + row, PLAIN + 16 * row] = 1.0
        back[:, 9 + row, PLAIN + 16 * row] = 1.0
    return send.astype(np.float32), along_x.astype(np.float32), back.astype(np.float32)


def mass_table():
    weights, _ = gll_tables()
    table = shift_mass * (weights[:, None] * weights[None, :]).reshape(N * N, 1)
    return np.broadcast_to(table, (N * N, 128)).astype(np.float32).copy()


def part(step, low, high, whole):
    return low if step < 0 else (high if step > 0 else whole)


def span(first, count, unit=1):
    return pl.ds(first * unit, count * unit)


def kernel(
    nx, ny, node_weights,
    sol_in, res_in, grains_in, schwarz_in, stiff_in, send_in, along_x_in, back_in, mass_in,
    sol_out, res_out, dir_out, steps_out,
    sol, ext0, ext1, grains, schwarz, stiff, send_table, along_x, back, mass,
    blk, oblk, ab, loc0, loc1, d, q1, z2, q2, r1, im2, lift, buf_y, buf_x, sv, sides, corners, sides1, corners1,
    load_sem, send_sem, recv_sem, gy_send, gy_recv, gx_send, gx_recv,
):
    x, y = lax.axis_index("gx"), lax.axis_index("gy")

    def inside(dx, dy):
        checks = []
        if dx > 0:
            checks.append(x < nx - 1)
        if dx < 0:
            checks.append(x > 0)
        if dy > 0:
            checks.append(y < ny - 1)
        if dy < 0:
            checks.append(y > 0)
        return functools.reduce(jnp.logical_and, checks)

    barrier = pltpu.get_barrier_semaphore()

    expected = jnp.int32(nx - 1 + ny - 1)
    for dx, dy in MOVES:
        there = inside(dx, dy)
        if dx and dy:
            expected = expected + there.astype(jnp.int32)

        @pl.when(there)
        def _():
            pl.semaphore_signal(barrier, inc=1, device_id=(x + dx, y + dy), device_id_type=MESH)

    @pl.loop(0, nx)
    def _(k):
        @pl.when((k > x + 1) | (k < x - 1))
        def _():
            pl.semaphore_signal(barrier, inc=1, device_id=(k, y), device_id_type=MESH)

    @pl.loop(0, ny)
    def _(k):
        @pl.when((k > y + 1) | (k < y - 1))
        def _():
            pl.semaphore_signal(barrier, inc=1, device_id=(x, k), device_id_type=MESH)

    loads = [
        pltpu.make_async_copy(src, dst, load_sem.at[i])
        for i, (src, dst) in enumerate(
            [
                (res_in.at[0, 0], ext0.at[pl.ds(1, N), pl.ds(N, N * N)]),
                (schwarz_in, schwarz.at[:, :, pl.ds(0, 512)]),
                (send_in.at[y], send_table),
                (along_x_in.at[x], along_x),
                (back_in.at[y], back),
                (grains_in.at[0], grains),
                (stiff_in, stiff.at[:, :, pl.ds(0, 512)]),
                (schwarz_in.at[:, :, pl.ds(0, 256)], schwarz.at[:, :, pl.ds(512, 256)]),
                (stiff_in.at[:, :, pl.ds(0, 256)], stiff.at[:, :, pl.ds(512, 256)]),
                (mass_in, mass),
                (sol_in.at[0, 0], sol),
            ]
        )
    ]
    for load in loads:
        load.start()

    for m, (dx, dy) in enumerate(MOVES):

        @pl.when(jnp.logical_not(inside(-dx, -dy)))
        def _():
            area = ext0.at[span(*part(dx, (N + 1, 1), (0, 1), (1, N))), span(*part(dy, (N + 1, 1), (0, 1), (1, N)), N)]
            area[...] = jnp.zeros_like(area)

    lane = lax.broadcasted_iota(jnp.int32, (1, 128), 1)
    last = 127
    row = lax.broadcasted_iota(jnp.int32, (N * N, 128), 0)
    wide = lax.broadcasted_iota(jnp.int32, (N * N, 128), 1)
    inner = lax.rem(row, N)
    shared_z = ((inner == 0) & (wide > 0)) | ((inner == N - 1) & (wide < last))
    weight_z = jnp.where(shared_z, 0.5, 1.0).astype(F32)
    low_y = jnp.where(y > 0, 0.5, 1.0).astype(F32)
    high_y = jnp.where(y < ny - 1, 0.5, 1.0).astype(F32)
    low_x = jnp.where(x > 0, 0.5, 1.0).astype(F32)
    high_x = jnp.where(x < nx - 1, 0.5, 1.0).astype(F32)
    weight_yz = weight_z * jnp.where(row < N, low_y, jnp.where(row >= N * N - N, high_y, 1.0))

    def from_below(v):
        return jnp.where(lane > 0, pltpu.roll(v, 1, axis=1), 0.0)

    def from_above(v):
        return jnp.where(lane < last, pltpu.roll(v, last, axis=1), 0.0)

    def total(v):
        return jnp.sum(jnp.sum(v, axis=0, keepdims=True), axis=1, keepdims=True)

    def weighted(product):
        middle = product(1)
        for a in range(2, N - 1):
            middle = middle + product(a)
        return weight_yz * (low_x * product(0) + middle + high_x * product(N - 1))

    own = pl.ds(N, N * N)

    def classes(field, weight, ends):
        middle = field(1)
        for a in range(2, N - 1):
            middle = middle + field(a)
        rows = []
        for scale, value in zip(ends, (field(0), middle, field(N - 1))):
            value = value * weight * scale
            inner_rows = value[N : 2 * N]
            for b in range(2, N - 1):
                inner_rows = inner_rows + value[b * N : b * N + N]
            for part_rows in (value[:N], inner_rows, value[N * N - N :]):
                rows.append(jnp.sum(part_rows, axis=0, keepdims=True))
        return rows

    def message(rows, *sums):
        result = jnp.zeros((1, 128), F32)
        for i, value in enumerate(rows):
            result = result + jnp.sum(value, axis=1, keepdims=True) * send_table[pl.ds(i, 1)]
        for i, value in enumerate(sums):
            result = result + total(value) * send_table[pl.ds(9 + i, 1)]
        return result

    loads[0].wait()
    loads[2].wait()
    first_message = total(weighted(lambda a: ext0[a + 1, own])) * send_table[pl.ds(4, 1)]
    pl.semaphore_wait(barrier, expected)

    def copies(phase, source, target):
        return [
            pltpu.make_async_remote_copy(
                src_ref=source(dx, dy),
                dst_ref=target(m),
                send_sem=send_sem.at[phase, m],
                recv_sem=recv_sem.at[phase, m],
                device_id=(x + dx, y + dy),
                device_id_type=MESH,
            )
            for m, (dx, dy) in enumerate(MOVES)
        ]

    def start(group, moves=LONGEST_FIRST):
        for m in moves:
            pl.when(inside(*MOVES[m]))(group[m].start)

    def arrive(group):
        for m, (dx, dy) in enumerate(MOVES):
            pl.when(inside(-dx, -dy))(group[m].wait_recv)

    def arrive_and_add(group, area, slot, scale=None):
        for m in NEAREST_FIRST:
            dx, dy = MOVES[m]

            @pl.when(inside(-dx, -dy))
            def _():
                group[m].wait_recv()
                target = area(dx, dy)
                value = incoming(*slot, m)[...]
                target[...] += value if scale is None else scale * value

    def sent(group):
        for m, (dx, dy) in enumerate(MOVES):
            pl.when(inside(dx, dy))(group[m].wait_send)

    def ext_target(m):
        dx, dy = MOVES[m]
        return ext0.at[span(*part(dx, (N + 1, 1), (0, 1), (1, N))), span(*part(dy, (N + 1, 1), (0, 1), (1, N)), N)]

    halo0 = copies(
        0,
        lambda dx, dy: res_in.at[
            0, 0, span(*part(dx, (1, 1), (N - 2, 1), (0, N))), span(*part(dy, (1, 1), (N - 2, 1), (0, N)), N)
        ],
        ext_target,
    )

    def stage(buffer, index, send, recv, count, device):
        def copy(k):
            return pltpu.make_async_remote_copy(
                src_ref=buffer.at[pl.ds(index, 1)],
                dst_ref=buffer.at[pl.ds(index, 1)],
                send_sem=send,
                recv_sem=recv,
                device_id=device(k),
                device_id_type=MESH,
            )

        @pl.loop(1, count)
        def _(k):
            copy(k).start()

    def all_rows(buffer, send, recv, count):
        rows = buffer.at[pl.ds(0, count - 1)]
        pltpu.make_async_copy(rows, rows, recv).wait()
        pltpu.make_async_copy(rows, rows, send).wait()

    def gather_y(g, value):
        buf_y[g, pl.ds(y, 1)] = value.reshape(1, 1, 128)
        stage(buf_y.at[g], y, gy_send.at[g], gy_recv.at[g], ny, lambda k: (x, lax.rem(y + k, ny)))

    def gather_x(g):
        all_rows(buf_y.at[g], gy_send.at[g], gy_recv.at[g], ny)
        value = jnp.sum(buf_y[g], axis=0)
        buf_x[g, pl.ds(x, 1)] = value.reshape(1, 1, 128)
        stage(buf_x.at[g], x, gx_send.at[g], gx_recv.at[g], nx, lambda k: (lax.rem(x + k, nx), y))

    def gathered(g):
        all_rows(buf_x.at[g], gx_send.at[g], gx_recv.at[g], nx)
        rows = buf_x[g].reshape(nx, 128)
        low, middle, high = (jnp.sum(rows * along_x[t], axis=0, keepdims=True) for t in range(3))
        row16 = lax.broadcasted_iota(jnp.int32, (16, 128), 0)
        value = jnp.where(row16 < 3, low, jnp.where(row16 < 6, middle, high))
        sums = jnp.sum(value * back[...], axis=1, keepdims=True)
        sv[g] = jnp.broadcast_to(sums, (16, 128))

    def lifted(g):
        for t in range(3):
            for s in range(3):
                at, count = ((0, 1), (1, N - 2), (N - 1, 1))[s]
                lift[t, pl.ds(at * N, count * N)] = jnp.broadcast_to(sv[g, pl.ds(3 * t + s, 1)], (count * N, 128))

    def product(matrix, v):
        high = v.astype(BF16)
        low = (v - high.astype(F32)).astype(BF16)
        return jnp.dot(matrix, jnp.concatenate([high, high, low], axis=0), preferred_element_type=F32)

    def solve(ext, loc, group):
        h = (N + 2) // 2
        for i in range(h):
            lower, upper = ext[i], ext[N + 1 - i]
            even, odd = lower + upper, lower - upper
            for j in range(h):
                one, two = slice(j * N, j * N + N), slice((N + 1 - j) * N, (N + 2 - j) * N)
                at = pl.ds((i * h + j) * N, N)
                blk[0, at] = even[one] + even[two]
                blk[1, at] = even[one] - even[two]
                blk[2, at] = odd[one] + odd[two]
                blk[3, at] = odd[one] - odd[two]
        count = h * h

        for p in range(4):
            source = blk.at[p]
            below = source[pl.ds(N - 2, count, stride=N)]
            above = source[pl.ds(1, count, stride=N)]
            source[pl.ds(count * N, count)] = from_below(below)
            source[pl.ds(count * (N + 1), count)] = from_above(above)
        for p in range(4):
            out = oblk.at[p]
            out[...] = product(schwarz[p], blk[p])
            first = out[pl.ds(0, count, stride=N)]
            final = out[pl.ds(N - 1, count, stride=N)]
            out[pl.ds(0, count, stride=N)] = first + from_below(final)
            out[pl.ds(N - 1, count, stride=N)] = final + from_above(first)
            out[pl.ds(1, count, stride=N)] += from_below(out[pl.ds(count * (N + 1), count)])
            out[pl.ds(N - 2, count, stride=N)] += from_above(out[pl.ds(count * N, count)])

        for i in range(h):
            if i == 2:
                start(group, LONGEST_FIRST[:6])
            for j in range(h):
                at = pl.ds((i * h + j) * N, N)
                ee, eo, oe, oo = oblk[0, at], oblk[1, at], oblk[2, at], oblk[3, at]
                one, two = pl.ds(j * N, N), pl.ds((N + 1 - j) * N, N)
                loc[i, one] = (ee + eo) + (oe + oo)
                loc[N + 1 - i, one] = (ee + eo) - (oe + oo)
                loc[i, two] = (ee - eo) + (oe - oo)
                loc[N + 1 - i, two] = (ee - eo) - (oe - oo)
        start(group, LONGEST_FIRST[6:])

    def spread_copies(phase, slot, loc):
        return copies(
            phase,
            lambda dx, dy: loc.at[
                span(*part(dx, (0, 2), (N, 2), (1, N))), span(*part(dy, (0, 2), (N, 2), (1, N)), N)
            ],
            lambda m: incoming(sides, corners, slot, m),
        )

    def node_area(field, dx, dy):
        return field.at[span(*part(dx, (N - 2, 2), (0, 2), (0, N))), span(*part(dy, (N - 2, 2), (0, 2), (0, N)), N)]

    porosity = None

    def apply(field, image, group=None):
        for a in range(N // 2):
            lower, upper = field[a], field[N - 1 - a]
            ab[0, pl.ds(a * N * N, N * N)] = lower + upper
            ab[1, pl.ds(a * N * N, N * N)] = lower - upper
        even = product(stiff[0], ab[0])
        odd = product(stiff[1], ab[1])
        for i in range(N // 2):
            at = slice(i * N * N, (i + 1) * N * N)
            scaled = mass[...] * F32(node_weights[i])
            image[i] = porosity * (even[at] + odd[at]) + scaled * field[i]
            image[N - 1 - i] = porosity * (even[at] - odd[at]) + scaled * field[N - 1 - i]
            for a in (i, N - 1 - i):
                first = image[a, pl.ds(0, N, stride=N)]
                final = image[a, pl.ds(N - 1, N, stride=N)]
                image[a, pl.ds(0, N, stride=N)] = first + from_below(final)
                image[a, pl.ds(N - 1, N, stride=N)] = final + from_above(first)
            if i == 1 and group is not None:
                start(group, LONGEST_FIRST[:6])
        if group is not None:
            start(group, LONGEST_FIRST[6:])

    gather_y(0, first_message)
    start(halo0)
    for p in range(4):
        blk[p, pl.ds(248, 8)] = jnp.zeros((8, 128), F32)
    for i, load in enumerate(loads):
        if i not in (0, 2):
            load.wait()
    porosity = 1.0 - 0.6 * grains[...].astype(F32) / MOST_GRAINS
    gather_x(0)
    arrive(halo0)
    spread0 = spread_copies(1, 0, loc0)
    solve(ext0, loc0, spread0)
    gathered(0)
    lifted(0)
    for a in range(N):
        d[a] = loc0[a + 1, own] + lift[0 if a == 0 else (2 if a == N - 1 else 1)]
    arrive_and_add(spread0, lambda dx, dy: node_area(d, dx, dy), (sides, corners, 0))

    faces = copies(
        2,
        lambda dx, dy: q1.at[
            span(*part(dx, (0, 2), (N - 2, 2), (0, N))), span(*part(dy, (0, 2), (N - 2, 2), (0, N)), N)
        ],
        lambda m: incoming(sides, corners, 1, m),
    )
    apply(d, q1, faces)
    rho1 = weighted(lambda a: ext0[a + 1, own] * d[a])
    curve = d[0] * q1[0]
    for a in range(1, N):
        curve = curve + d[a] * q1[a]
    gather_y(1, message(classes(lambda a: q1[a], weight_z, (1.0, 1.0, 1.0)), rho1, weight_z * curve))
    for i in (0, N + 1):
        ext1[i] = jnp.zeros_like(ext1[i])
    for a in range(N):
        ext1[a + 1, pl.ds(0, N)] = jnp.zeros((N, 128), F32)
        ext1[a + 1, own] = q1[a]
        ext1[a + 1, pl.ds(N * N + N, N)] = jnp.zeros((N, 128), F32)
    gather_x(1)
    arrive_and_add(
        faces,
        lambda dx, dy: ext1.at[span(*part(dx, (N, 2), (0, 2), (1, N))), span(*part(dy, (N, 2), (0, 2), (1, N)), N)],
        (sides, corners, 1),
    )

    spread1 = spread_copies(3, 2, loc1)
    solve(ext1, loc1, spread1)
    gathered(1)
    lifted(1)
    rho1, curve1 = sv[1, pl.ds(9, 1)], sv[1, pl.ds(10, 1)]
    step1 = rho1 / curve1
    for a in range(N):
        z2[a] = d[a] - step1 * (loc1[a + 1, own] + lift[0 if a == 0 else (2 if a == N - 1 else 1)])
        r1[a] = ext0[a + 1, own] - step1 * ext1[a + 1, own]
        sol[a] = sol[a] + step1 * d[a]
    arrive_and_add(spread1, lambda dx, dy: node_area(z2, dx, dy), (sides, corners, 2), -step1)

    rho2 = jnp.sum(weighted(lambda a: r1[a] * z2[a]), axis=0, keepdims=True)
    curve_mixed = z2[0] * q1[0]
    for a in range(1, N):
        curve_mixed = curve_mixed + z2[a] * q1[a]
    curve_mixed = jnp.sum(weight_z * curve_mixed, axis=0, keepdims=True)
    apply(z2, q2)
    curve_new = z2[0] * q2[0]
    for a in range(1, N):
        curve_new = curve_new + z2[a] * q2[a]
    gather_y(2, message([], rho2, weight_z * curve_new, curve_mixed))
    edges = copies(
        4,
        lambda dx, dy: q2.at[
            span(*part(dx, (0, 1), (N - 1, 1), (0, N))), span(*part(dy, (0, 1), (N - 1, 1), (0, N)), N)
        ],
        lambda m: incoming(sides1, corners1, None, m),
    )
    start(edges)
    for a in range(N):
        im2[a] = q2[a]
    gather_x(2)
    arrive_and_add(
        edges,
        lambda dx, dy: im2.at[
            span(*part(dx, (N - 1, 1), (0, 1), (0, N))), span(*part(dy, (N - 1, 1), (0, 1), (0, N)), N)
        ],
        (sides1, corners1, None),
    )
    for group in (halo0, spread0, faces, spread1, edges):
        sent(group)
    all_rows(buf_x.at[2], gx_send.at[2], gx_recv.at[2], nx)
    value = jnp.sum(buf_x[2], axis=0)
    rho2, curve_new, curve_mixed = (
        jnp.sum(jnp.where(lane == PLAIN + 16 * i, value, 0.0), axis=1, keepdims=True) for i in range(3)
    )
    ratio = rho2 / rho1
    step2 = rho2 / (curve_new + ratio * (2.0 * curve_mixed + ratio * curve1))
    for a in range(N):
        direction = z2[a] + ratio * d[a]
        dir_out[0, 0, a] = direction
        sol_out[0, 0, a] = sol[a] + step2 * direction
        res_out[0, 0, a] = r1[a] - step2 * (im2[a] + ratio * ext1[a + 1, own])
    steps_out[0] = step1[0, 0]
    steps_out[1] = step2[0, 0]


def deliver(sol, res, direction, steps, sol_out, res_out, dir_out, steps_out, sems):
    copies = [
        pltpu.make_async_copy(src, dst, sems.at[i])
        for i, (src, dst) in enumerate(
            ((steps, steps_out), (sol, sol_out), (res, res_out), (direction, dir_out))
        )
    ]
    for copy in copies:
        copy.start()
    for copy in copies:
        copy.wait()


def incoming(sides, corners, slot, m):
    first, second = MOVES[m]
    if first and second:
        return corners.at[m - 4] if slot is None else corners.at[slot, m - 4]
    which = 0 if first else 1
    ref = sides[which]
    return ref.at[m % 2] if slot is None else ref.at[slot, m % 2]


def solution(mesh):
    nx, ny = mesh.shape["gx"], mesh.shape["gy"]
    weights, _ = gll_tables()
    send, along_x, back = coarse_tables(nx, ny, 128)
    schwarz, stiff, mass = schwarz_blocks(), stiffness_blocks(), mass_table()
    nn = N * N
    field = pltpu.VMEM((N, nn, 128), F32)
    wide = pltpu.VMEM((N + 2, nn + 2 * N, 128), F32)
    vmem, anywhere = pl.BlockSpec(memory_space=pltpu.VMEM), pl.BlockSpec(memory_space=pl.ANY)
    smem = pl.BlockSpec(memory_space=pltpu.SMEM)

    def step(sol, res, grains):
        shape = sol.shape
        flat = (1, 1, N, nn, 128)
        out = jax.ShapeDtypeStruct(flat, F32)
        outs = pl.pallas_call(
            functools.partial(kernel, nx, ny, [float(v) for v in weights]),
            out_shape=(out, out, out, jax.ShapeDtypeStruct((2,), F32)),
            in_specs=[anywhere] * 9,
            out_specs=(vmem, vmem, vmem, smem),
            scratch_shapes=[
                field, wide, wide,
                pltpu.VMEM((1, 128), jnp.int32),
                pltpu.VMEM((4, 256, 768), BF16),
                pltpu.VMEM((2, 256, 768), BF16),
                pltpu.VMEM((16, 128), F32),
                pltpu.VMEM((3, nx, 128), F32),
                pltpu.VMEM((16, 128), F32),
                pltpu.VMEM((nn, 128), F32),
                pltpu.VMEM((4, 256, 128), F32),
                pltpu.VMEM((4, 256, 128), F32),
                pltpu.VMEM((2, 256, 128), F32),
                wide, wide, field, field, field, field, field, field,
                pltpu.VMEM((3, nn, 128), F32),
                pltpu.VMEM((3, ny, 1, 128), F32),
                pltpu.VMEM((3, nx, 1, 128), F32),
                pltpu.VMEM((3, 16, 128), F32),
                [pltpu.VMEM((3, 2, 2, nn, 128), F32), pltpu.VMEM((3, 2, N, 2 * N, 128), F32)],
                pltpu.VMEM((3, 4, 2, 2 * N, 128), F32),
                [pltpu.VMEM((2, 1, nn, 128), F32), pltpu.VMEM((2, N, N, 128), F32)],
                pltpu.VMEM((4, 1, N, 128), F32),
                pltpu.SemaphoreType.DMA((11,)),
                pltpu.SemaphoreType.DMA((5, 8)),
                pltpu.SemaphoreType.DMA((5, 8)),
                pltpu.SemaphoreType.DMA((3,)),
                pltpu.SemaphoreType.DMA((3,)),
                pltpu.SemaphoreType.DMA((3,)),
                pltpu.SemaphoreType.DMA((3,)),
            ],
            compiler_params=pltpu.CompilerParams(collective_id=0, has_side_effects=True, vmem_limit_bytes=40 * 1024 * 1024),
            name="cg_steps",
        )(
            *(pltpu.with_memory_space_constraint(v, pltpu.HBM) for v in (
            sol.reshape(flat), res.reshape(flat), grains,
            jnp.asarray(schwarz), jnp.asarray(stiff), jnp.asarray(send), jnp.asarray(along_x),
            jnp.asarray(back), jnp.asarray(mass),))
        )
        hbm = pl.BlockSpec(memory_space=pltpu.HBM)
        outs = pl.pallas_call(
            deliver,
            out_shape=(out, out, out, jax.ShapeDtypeStruct((2,), F32)),
            in_specs=[anywhere] * 4,
            out_specs=(hbm,) * 4,
            scratch_shapes=[pltpu.SemaphoreType.DMA((4,))],
            compiler_params=pltpu.CompilerParams(vmem_limit_bytes=2 * 1024 * 1024),
            name="deliver",
        )(*outs)
        return tuple(v.reshape(shape) for v in outs[:3]) + (outs[3],)

    wide_spec = P("gx", "gy", None, None, None, None)
    return jax.shard_map(
        step,
        mesh=mesh,
        in_specs=(wide_spec, wide_spec, P("gx", "gy", None)),
        out_specs=(wide_spec, wide_spec, wide_spec, P()),
        check_vma=False,
    )
```
